128 devices in a mesh: dp: 4 (over y), expert: 32 (over x, z, core).
Axes of the slice: x: 4, y: 4, z: 4, core: 2. Of those that a mesh axis runs over, the one named last changes fastest.
Arguments:
- tokens: bfloat16 [8192, 4096], P(('dp', 'expert')), may hold values from -6 to 6
- routes: int32 [8192, 8], P(('dp', 'expert')), may hold values from 0 to 63, all different within a row; in each aligned block of 64 rows (0 to 63, 64 to 127, ...) at most 12 rows name the same one
- gate_fixed: int32 [8192, 8], P(('dp', 'expert')), may hold values from 1 to 65535
- w_gate: bfloat16 [128, 4096, 768], P(('dp', 'expert')), may hold values from -0.09375 to 0.09375
- w_up: bfloat16 [128, 4096, 768], P(('dp', 'expert')), may hold values from -0.09375 to 0.09375
- w_down: bfloat16 [128, 768, 4096], P(('dp', 'expert')), may hold values from -0.15625 to 0.15625
Outputs:
- mixed: bfloat16 [8192, 4096], P(('dp', 'expert'))
The draws below stay inside these ranges and needn't reach their ends.
Inputs may be any that keep to these rules, and one draw needn't show every extreme that they name: `routes`: each row names 8 different experts. In each aligned block of 64 rows (the rows of one device) no expert is named by more than 12 rows, and in some block one expert is named by exactly 12 rows.
All inputs are finite; a program needn't handle non-finite values.
Results may differ from the reference program's by a relative error of at most 0.0058.
Values may be sent and summed in bfloat16 or wider, within the bound.
A program may use at most 192 MiB of HBM per device.

```python
import math
import jax
import jax.numpy as jnp
import numpy as np
from jax import lax

D = 4096
FF = 1536
TOP = 8
TOK_DEV = 64
HALF = 768
EXPERTS = 64
CAP = 12
TOKENS = 8192
N_DP = 4
N_EXPERT = 32


def with_ends(array, key, smallest, high):
    index_at = [jax.random.randint(jax.random.fold_in(key, axis), (), 0, length) for axis, length in enumerate(array.shape)]
    widest = array.shape.index(max(array.shape))
    next_to = index_at[:widest] + [(index_at[widest] + 1) % array.shape[widest]] + index_at[widest + 1:]
    return array.at[tuple(index_at)].set(smallest).at[tuple(next_to)].set(high)


def block_levels(own_key, extent, shards, smallest, high):
    factor_of = 1.0
    for axis_at, blocks in shards:
        draws = jax.random.uniform(jax.random.fold_in(jax.random.fold_in(own_key, 6), axis_at), (blocks,), jnp.float32, smallest / len(shards), high / len(shards))
        factor_of = factor_of * jnp.repeat(jnp.exp(draws), extent[axis_at] // blocks).reshape((-1,) + (1,) * (len(extent) - 1 - axis_at))
    return factor_of


def assign_block(rng, own, number, rows, count, top, reach, lean):
    ranking = jax.random.permutation(rng, count)
    packed, usual = shares(count, rows * top, reach, lean, True), shares(count, rows * top, reach, lean, False)
    places = jnp.arange(count)

    def named(sizes, turn):
        used = int((sizes > 0).sum())
        fixed = max(1, used // 4)
        moved = fixed + (places - fixed + turn * (used - fixed)) % max(1, count - fixed)
        return jnp.zeros((count,), jnp.int32).at[ranking[jnp.where(places < fixed, places, moved)]].set(jnp.asarray(sizes, jnp.int32))

    sizes = jnp.where(number % 4 == 0, named(packed, number // 4), named(usual, number - number // 4 - 1))
    mixed = jax.random.permutation(jax.random.fold_in(own, 3), count)
    donor, sink = mixed[0:count // 2 * 2:2], mixed[1:count // 2 * 2:2]
    slack = jnp.minimum(sizes[donor] - 1, reach - sizes[sink]) // 2
    slack = jnp.where((donor == ranking[0]) | (sink == ranking[0]) | (sizes[sink] == 0), 0, jnp.maximum(slack, 0))
    moved = jax.random.randint(jax.random.fold_in(own, 4), (count // 2,), 0, 1 << 20) % (slack + 1)
    sizes = sizes.at[donor].add(-moved).at[sink].add(moved)
    items = jnp.searchsorted(jnp.cumsum(sizes), jnp.arange(rows * top), side="right").astype(jnp.int32)
    table = items.reshape(top, rows).T
    table = table[jax.random.permutation(jax.random.fold_in(own, 1), rows)]
    turn = jax.random.randint(jax.random.fold_in(own, 2), (rows, 1), 0, top)
    return jnp.take_along_axis(table, (jnp.arange(top)[None, :] + turn) % top, axis=1)


def shares(amount, total, reach, skew, full):
    weights = [(1 << 20) // math.isqrt(standing ** skew) + 1 for standing in range(1, amount + 1)]
    largest = reach if full else min(reach, max(-(-total // amount), total * weights[0] // sum(weights)))
    least = 1 if total - largest >= amount - 1 else 0
    holding, spare = [largest] + [least] * (amount - 1), total - largest - least * (amount - 1)
    while spare > 0:
        candidates = [i for i in range(1, amount) if holding[i] < largest] or [i for i in range(1, amount) if holding[i] < reach]
        mass, budget = sum([weights[i] for i in candidates]), spare
        for i in candidates:
            extra = min(reach - holding[i], max(1, budget * weights[i] // mass), spare)
            holding[i] = holding[i] + extra
            spare = spare - extra
    return np.array(holding)


def normal_values(rng, extent, deviation, bound, shards=(), held_as=jnp.bfloat16):
    level = block_levels(rng, extent, shards, -0.22, 0.18) if shards else 1.0
    values = jax.random.normal(rng, extent, jnp.float32) * deviation * level
    return jnp.minimum(jnp.maximum(values, -bound), bound).astype(held_as)


def setup_inputs(seed: int = 0) -> dict:
    keys = jax.random.split(jax.random.key(seed), 7)
    tokens = normal_values(keys[0], (TOKENS, D), 1.0, 6.0, ((0, 128),))
    routes_keys = jax.random.split(jax.random.fold_in(keys[1], 1), TOKENS // TOK_DEV)
    routes_turns = jax.random.permutation(jax.random.fold_in(keys[1], 3), TOKENS // TOK_DEV)
    routes = jax.vmap(lambda own, number: assign_block(jax.random.fold_in(keys[1], 2), own, number, TOK_DEV, EXPERTS, TOP, CAP, 2))(routes_keys, routes_turns).reshape((TOKENS, TOP))
    gate_fixed = with_ends(jax.random.randint(keys[2], (TOKENS, TOP), 1, 65536), jax.random.fold_in(keys[2], 1), 1, 65535).astype(jnp.int32)
    w_gate = normal_values(keys[3], (2 * EXPERTS, D, HALF), D ** -0.5, 0.09375, ((0, 128),))
    w_up = normal_values(keys[4], (2 * EXPERTS, D, HALF), D ** -0.5, 0.09375, ((0, 128),))
    w_down = normal_values(keys[5], (2 * EXPERTS, HALF, D), FF ** -0.5, 0.15625, ((0, 128),))
    return {"tokens": tokens, "routes": routes, "gate_fixed": gate_fixed, "w_gate": w_gate, "w_up": w_up, "w_down": w_down}


def reference(tokens, routes, gate_fixed, w_gate, w_up, w_down):
    sources = N_DP * N_EXPERT
    quant = gate_fixed.astype(jnp.float32)
    weights = quant / jnp.sum(quant, axis=1, keepdims=True)
    blocks = routes.reshape(sources, TOK_DEV * TOP)
    onehot = (blocks[:, :, None] == jnp.arange(EXPERTS, dtype=jnp.int32)[None, None, :]).astype(jnp.int32)
    before = jnp.cumsum(onehot, axis=1) - onehot
    slot = jnp.sum(before * onehot, axis=2)
    source_ids = jnp.arange(sources, dtype=jnp.int32)[:, None]
    place = (blocks * sources + source_ids) * CAP + slot
    token_ids = source_ids * TOK_DEV + (jnp.arange(TOK_DEV * TOP, dtype=jnp.int32) // TOP)[None, :]
    table = jnp.full((EXPERTS * sources * CAP,), TOKENS, jnp.int32).at[place.reshape(-1)].set(token_ids.reshape(-1))
    factor = jnp.zeros((EXPERTS * sources * CAP,), jnp.float32).at[place.reshape(-1)].set(weights.reshape(-1))
    padded = jnp.concatenate([tokens, jnp.zeros((1, D), tokens.dtype)], axis=0)
    gate_pairs = w_gate.reshape(EXPERTS, 2, D, HALF)
    up_pairs = w_up.reshape(EXPERTS, 2, D, HALF)
    down_pairs = w_down.reshape(EXPERTS, 2, HALF, D)

    def one_expert(total, items):
        index, scale, gate_pair, up_pair, down_pair = items
        rows = padded[index]
        gate_full = jnp.concatenate([gate_pair[0], gate_pair[1]], axis=1)
        up_full = jnp.concatenate([up_pair[0], up_pair[1]], axis=1)
        down_full = jnp.concatenate([down_pair[0], down_pair[1]], axis=0)
        gate = jnp.dot(rows, gate_full, preferred_element_type=jnp.float32)
        upper = jnp.dot(rows, up_full, preferred_element_type=jnp.float32)
        hidden = (jax.nn.silu(gate) * upper).astype(jnp.bfloat16)
        result = jnp.dot(hidden, down_full, preferred_element_type=jnp.float32).astype(jnp.bfloat16)
        total = total.at[index].add(scale[:, None] * result.astype(jnp.float32))
        return total, None

    start = jnp.zeros((TOKENS + 1, D), jnp.float32)
    items = (table.reshape(EXPERTS, sources * CAP), factor.reshape(EXPERTS, sources * CAP), gate_pairs, up_pairs, down_pairs)
    total, _ = lax.scan(one_expert, start, items)
    return total[:TOKENS].astype(jnp.bfloat16)
```

```python
import functools

import jax
import jax.numpy as jnp
from jax import lax
from jax.experimental import pallas as pl
from jax.experimental.pallas import tpu as pltpu
from jax.sharding import PartitionSpec as P

MESH = pl.DeviceIdType.MESH
F32 = jnp.float32
BF16 = jnp.bfloat16

SIDE = 4
TOK = 64
TOP = 8
CAP = 12
EXPERTS = 64
WIDTH = 4096
HALF = 768
BLOCK = SIDE * CAP
PIECE = SIDE * BLOCK
ROWS = SIDE * PIECE

PARTS = ((0, 1408), (1408, 1408), (2816, 1280))
ORDERS = ("yxz", "xzy", "zyx")
STEPS = (1, 3, 2)


def twelfth(index):
    return (index * 5462) >> 16


def nt(left, right):
    return lax.dot_general(left, right, (((1,), (1,)), ((), ())), preferred_element_type=F32)


def swap_matrix():
    row = lax.broadcasted_iota(jnp.int32, (PIECE, PIECE), 0)
    col = lax.broadcasted_iota(jnp.int32, (PIECE, PIECE), 1)
    pair = twelfth(row)
    source = ((pair & 3) * SIDE + (pair >> 2)) * CAP + (row - pair * CAP)
    return (source == col).astype(F32).astype(BF16)


def kernel(
    x_ref,
    routes_ref,
    gate_ref,
    wg_hbm,
    wu_hbm,
    wd_hbm,
    out_ref,
    mid_ref,
    back_ref,
    home_ref,
    lines,
    tables,
    packed,
    landed,
    hidden,
    turned,
    wg,
    wu,
    wd,
    sums,
    sem_send,
    sem_recv,
    tab_send,
    tab_recv,
    w_send,
    w_recv,
    w_local,
    own_sem,
):
    row = lax.axis_index("expert")
    at = {"y": lax.axis_index("dp"), "x": row // 8, "z": (row // 2) % 4}
    core = row % 2

    def device(where, which):
        return (where["y"], (where["x"] * 4 + where["z"]) * 2 + which)

    def peer(axis, shift):
        where = dict(at)
        where[axis] = (at[axis] + shift) % SIDE
        return device(where, core)

    partner = device(at, 1 - core)

    barrier = pltpu.get_barrier_semaphore()
    for axis in "yxz":
        for shift in STEPS:
            pl.semaphore_signal(barrier, inc=1, device_id=peer(axis, shift), device_id_type=MESH)
    pl.semaphore_signal(barrier, inc=1, device_id=partner, device_id_type=MESH)
    pl.semaphore_wait(barrier, 10)

    def remote(phase, part, step, src, dst, target):
        return pltpu.make_async_remote_copy(
            src_ref=src,
            dst_ref=dst,
            send_sem=sem_send.at[phase, part, step],
            recv_sem=sem_recv.at[phase, part, step],
            device_id=target,
            device_id_type=MESH,
        )

    def cols(part):
        return pl.ds(PARTS[part][0], PARTS[part][1])

    def phase0(part, step):
        dst = lines.at[pl.ds(step * TOK, TOK), cols(part)]
        return remote(0, part, step, x_ref.at[:, cols(part)], dst, peer(ORDERS[part][0], -step))

    for step in STEPS:
        for part in range(3):
            phase0(part, step).start()

    expert = lax.broadcasted_iota(jnp.int32, (TOK, EXPERTS), 1)
    quant = gate_ref[...].astype(F32)
    weight = quant / jnp.sum(quant, axis=1, keepdims=True)
    named = jnp.zeros((TOK, EXPERTS), F32)
    share = jnp.zeros((TOK, EXPERTS), F32)
    for k in range(TOP):
        hit = routes_ref[:, k : k + 1] == expert
        named = named + jnp.where(hit, 1.0, 0.0)
        share = share + jnp.where(hit, weight[:, k : k + 1], 0.0)
    earlier = (
        lax.broadcasted_iota(jnp.int32, (TOK, TOK), 1) < lax.broadcasted_iota(jnp.int32, (TOK, TOK), 0)
    ).astype(F32).astype(BF16)
    before = jnp.dot(earlier, named.astype(BF16), preferred_element_type=F32)
    slots = jnp.where(named > 0.5, before, -1.0)
    own_table = jnp.concatenate([slots, share], axis=1).astype(BF16)
    for part in range(3):
        tables[part, 0:TOK, :] = own_table

    def table_copy(part, step):
        return pltpu.make_async_remote_copy(
            src_ref=tables.at[part, pl.ds(0, TOK)],
            dst_ref=tables.at[part, pl.ds(step * TOK, TOK)],
            send_sem=tab_send.at[part, step],
            recv_sem=tab_recv.at[part, step],
            device_id=peer(ORDERS[part][0], -step),
            device_id_type=MESH,
        )

    for step in STEPS:
        for part in range(3):
            table_copy(part, step).start()

    def weight_copies():
        copies = []
        for index, (src, dst) in enumerate(((wg_hbm, wg), (wu_hbm, wu), (wd_hbm, wd))):
            copies.append(pltpu.make_async_copy(src.at[0], dst.at[0], w_local.at[index]))
            copies.append(
                pltpu.make_async_remote_copy(
                    src_ref=src.at[0],
                    dst_ref=dst.at[1],
                    send_sem=w_send.at[index],
                    recv_sem=w_recv.at[index],
                    device_id=partner,
                    device_id_type=MESH,
                )
            )
        return copies

    for copy in weight_copies():
        copy.start()

    lines[0:TOK, :] = x_ref[...]
    for step in STEPS:
        for part in range(3):
            phase0(part, step).wait()
            table_copy(part, step).wait()

    def chooser(part, rows, first, dim):
        index = first + lax.broadcasted_iota(jnp.int32, rows, dim)
        chunk = twelfth(index)
        slot = index - chunk * CAP
        member = chunk & 3
        dc = (chunk >> 2) & 3
        db = chunk >> 4
        a, b, c = (at[axis] for axis in ORDERS[part])
        where = dict(zip(ORDERS[part], (a, (b - db) & 3, (c - dc) & 3)))
        return where["y"] * 16 + where["x"] * 4 + where["z"], member, slot

    def phase1(part, step):
        return remote(
            1,
            part,
            step,
            packed.at[step, :, :, cols(part)],
            mid_ref.at[:, step, :, cols(part)],
            peer(ORDERS[part][1], -step),
        )

    def phase1_own(part):
        return pltpu.make_async_copy(
            packed.at[0, :, :, cols(part)], mid_ref.at[:, 0, :, cols(part)], own_sem.at[0, part]
        )

    for step in (1, 3, 2, 0):
        for part in range(3):
            start, size = PARTS[part]
            named_expert, _, _ = chooser(part, (PIECE, EXPERTS), step * PIECE, 0)
            chosen = (
                named_expert == lax.broadcasted_iota(jnp.int32, (PIECE, EXPERTS), 1)
            ).astype(F32).astype(BF16)
            found = nt(chosen, tables[part, :, 0:EXPERTS])
            _, member, slot = chooser(part, (PIECE, SIDE * TOK), step * PIECE, 0)
            holder = lax.broadcasted_iota(jnp.int32, (PIECE, SIDE * TOK), 1) >> 6
            pick = jnp.where((found == slot.astype(F32)) & (holder == member), 1.0, 0.0).astype(BF16)
            rows = jnp.dot(pick, lines[:, start : start + size], preferred_element_type=F32)
            packed[step, :, :, start : start + size] = rows.astype(BF16).reshape(SIDE, BLOCK, size)
            if step:
                phase1(part, step).start()
            else:
                phase1_own(part).start()

    def phase2(part, step):
        return remote(
            2,
            part,
            step,
            mid_ref.at[step, :, :, cols(part)],
            landed.at[step, :, :, cols(part)],
            peer(ORDERS[part][2], -step),
        )

    def phase2_own(part):
        return pltpu.make_async_copy(
            mid_ref.at[0, :, :, cols(part)], landed.at[0, :, :, cols(part)], own_sem.at[1, part]
        )

    for part in range(3):
        phase1_own(part).wait()
    for step in STEPS:
        for part in range(3):
            phase1(part, step).wait()
    for step in STEPS:
        for part in range(3):
            phase2(part, step).start()
    for part in range(3):
        phase2_own(part).start()

    swap = swap_matrix()

    for copy in weight_copies():
        copy.wait()
    for part in range(3):
        phase2_own(part).wait()
    for step in STEPS:
        for part in range(3):
            phase2(part, step).wait()

    start, size = PARTS[0]
    packed[:, :, :, start : start + size] = landed[:, :, :, start : start + size]
    start, size = PARTS[1]
    for dz in range(SIDE):
        part_rows = landed[:, dz, :, start : start + size].reshape(PIECE, size)
        ordered = jnp.dot(swap, part_rows, preferred_element_type=F32).astype(BF16)
        packed[dz, :, :, start : start + size] = ordered.reshape(SIDE, BLOCK, size)
    start, size = PARTS[2]
    for dx in range(SIDE):
        part_rows = landed[dx, :, :, start : start + size].reshape(PIECE, size)
        ordered = jnp.dot(swap, part_rows, preferred_element_type=F32).astype(BF16)
        packed[:, dx, :, start : start + size] = ordered.reshape(SIDE, BLOCK, size)

    chunk = 256
    for side in range(2):

        @pl.loop(0, HALF // chunk)
        def _(index):
            these = pl.ds(pl.multiple_of(index * chunk, chunk), chunk)
            those = pl.ds(pl.multiple_of(side * HALF + index * chunk, chunk), chunk)
            for half in range(2):
                rows = packed[2 * half : 2 * half + 2].reshape(ROWS // 2, WIDTH)
                gate = jnp.dot(rows, wg[side, :, these], preferred_element_type=F32)
                upper = jnp.dot(rows, wu[side, :, these], preferred_element_type=F32)
                value = (gate / (1.0 + jnp.exp(-gate)) * upper).astype(BF16)
                hidden[2 * half : 2 * half + 2, :, :, those] = value.reshape(2, SIDE, BLOCK, chunk)

    def phase3(part, step):
        return remote(
            3,
            part,
            step,
            landed.at[step, :, :, cols(part)],
            back_ref.at[:, step, :, cols(part)],
            peer(ORDERS[part][2], step),
        )

    def phase3_own(part):
        return pltpu.make_async_copy(
            landed.at[0, :, :, cols(part)], back_ref.at[:, 0, :, cols(part)], own_sem.at[2, part]
        )

    for part in range(3):
        start, size = PARTS[part]
        if part == 1:
            for dz in range(SIDE):
                rows = hidden[dz].reshape(PIECE, 2 * HALF)
                ordered = jnp.dot(swap, rows, preferred_element_type=F32).astype(BF16)
                turned[:, dz] = ordered.reshape(SIDE, BLOCK, 2 * HALF)
        if part == 2:
            for dx in range(SIDE):
                rows = hidden[:, dx].reshape(PIECE, 2 * HALF)
                ordered = jnp.dot(swap, rows, preferred_element_type=F32).astype(BF16)
                turned[dx] = ordered.reshape(SIDE, BLOCK, 2 * HALF)
        source = hidden if part == 0 else turned
        for half in range(2):
            rows = source[2 * half : 2 * half + 2].reshape(ROWS // 2, 2 * HALF)
            for first in range(start, start + size, 256):
                wide = min(256, start + size - first)
                total = jnp.dot(rows[:, :HALF], wd[0, :, first : first + wide], preferred_element_type=F32)
                total = total + jnp.dot(
                    rows[:, HALF:], wd[1, :, first : first + wide], preferred_element_type=F32
                )
                landed[2 * half : 2 * half + 2, :, :, first : first + wide] = total.astype(BF16).reshape(
                    2, SIDE, BLOCK, wide
                )
        for step in STEPS:
            phase3(part, step).start()
        phase3_own(part).start()

    def phase4(part, step):
        return remote(
            4,
            part,
            step,
            back_ref.at[step, :, :, cols(part)],
            home_ref.at[step, :, :, cols(part)],
            peer(ORDERS[part][1], step),
        )

    def phase4_own(part):
        return pltpu.make_async_copy(
            back_ref.at[0, :, :, cols(part)], packed.at[0, :, :, cols(part)], own_sem.at[3, part]
        )

    def load_home(part, step):
        return pltpu.make_async_copy(
            home_ref.at[step, :, :, cols(part)], packed.at[step, :, :, cols(part)], own_sem.at[3 + step, part]
        )

    for part in range(3):
        phase3_own(part).wait()
        for step in STEPS:
            phase3(part, step).wait()
        for step in STEPS:
            phase4(part, step).start()
        phase4_own(part).start()

    def phase5(part, step):
        return remote(
            5,
            part,
            step,
            lines.at[pl.ds(step * TOK, TOK), cols(part)],
            sums.at[pl.ds(step * TOK, TOK), cols(part)],
            peer(ORDERS[part][0], step),
        )

    for part in range(3):
        start, size = PARTS[part]
        named_expert, _, _ = chooser(part, (ROWS, EXPERTS), 0, 0)
        chosen = (
            named_expert == lax.broadcasted_iota(jnp.int32, (ROWS, EXPERTS), 1)
        ).astype(F32).astype(BF16)
        found = nt(tables[part, :, 0:EXPERTS], chosen)
        scale = nt(tables[part, :, EXPERTS : 2 * EXPERTS], chosen)
        _, member, slot = chooser(part, (SIDE * TOK, ROWS), 0, 1)
        holder = lax.broadcasted_iota(jnp.int32, (SIDE * TOK, ROWS), 0) >> 6
        mix = jnp.where((found == slot.astype(F32)) & (holder == member), scale, 0.0).astype(BF16)
        for step in STEPS:
            phase4(part, step).wait()
        for step in STEPS:
            load_home(part, step).start()
        phase4_own(part).wait()
        for step in STEPS:
            load_home(part, step).wait()
        for first in range(start, start + size, 256):
            wide = min(256, start + size - first)
            rows = packed[:, :, :, first : first + wide].reshape(ROWS, wide)
            lines[:, first : first + wide] = jnp.dot(mix, rows, preferred_element_type=F32).astype(BF16)
        for step in STEPS:
            phase5(part, step).start()

    for part in range(3):
        start, size = PARTS[part]
        for step in STEPS:
            phase5(part, step).wait()
        total = lines[0:TOK, start : start + size].astype(F32)
        for step in STEPS:
            total = total + sums[step * TOK : (step + 1) * TOK, start : start + size].astype(F32)
        out_ref[:, start : start + size] = total.astype(BF16)


def on_device(tokens, routes, gate_fixed, w_gate, w_up, w_down):
    big = jax.ShapeDtypeStruct((SIDE, SIDE, BLOCK, WIDTH), BF16)
    vmem = pl.BlockSpec(memory_space=pltpu.VMEM)
    hbm = pl.BlockSpec(memory_space=pltpu.HBM)
    dma = pltpu.SemaphoreType.DMA
    out, _, _, _ = pl.pallas_call(
        kernel,
        out_shape=(jax.ShapeDtypeStruct((TOK, WIDTH), BF16), big, big, big),
        in_specs=[vmem, vmem, vmem, hbm, hbm, hbm],
        out_specs=(vmem, hbm, hbm, hbm),
        scratch_shapes=[
            pltpu.VMEM((SIDE * TOK, WIDTH), BF16),
            pltpu.VMEM((3, SIDE * TOK, 2 * EXPERTS), BF16),
            pltpu.VMEM((SIDE, SIDE, BLOCK, WIDTH), BF16),
            pltpu.VMEM((SIDE, SIDE, BLOCK, WIDTH), BF16),
            pltpu.VMEM((SIDE, SIDE, BLOCK, 2 * HALF), BF16),
            pltpu.VMEM((SIDE, SIDE, BLOCK, 2 * HALF), BF16),
            pltpu.VMEM((2, WIDTH, HALF), BF16),
            pltpu.VMEM((2, WIDTH, HALF), BF16),
            pltpu.VMEM((2, HALF, WIDTH), BF16),
            pltpu.VMEM((SIDE * TOK, WIDTH), BF16),
            dma((6, 3, SIDE)),
            dma((6, 3, SIDE)),
            dma((3, SIDE)),
            dma((3, SIDE)),
            dma((3,)),
            dma((3,)),
            dma((3,)),
            dma((7, 3)),
        ],
        compiler_params=pltpu.CompilerParams(
            collective_id=0, has_side_effects=True, vmem_limit_bytes=67043328
        ),
        name="moe",
    )(tokens, routes, gate_fixed, w_gate, w_up, w_down)
    return out


def solution(mesh):
    split = P(("dp", "expert"), None)
    placed = (split, split, split) + (P(("dp", "expert"), None, None),) * 3
    return jax.shard_map(on_device, mesh=mesh, in_specs=placed, out_specs=split, check_vma=False)
```

```python
import jax
import jax.numpy as jnp
from jax import lax
from jax.experimental import pallas as pl
from jax.experimental.pallas import tpu as pltpu
from jax.sharding import PartitionSpec as P

MESH = pl.DeviceIdType.MESH
F32 = jnp.float32
BF16 = jnp.bfloat16

SIDE = 4
TOK = 64
TOP = 8
EXPERTS = 64
WIDTH = 4096
HALF = 768
GROUPS = 3
SLOTS = 4
BLOCK = SIDE * SLOTS
ROWS = SIDE * SIDE * BLOCK

PARTS = ((0, 1408), (1408, 1408), (2816, 1280))
ORDERS = ("yxz", "xzy", "zyx")
STEPS = (1, 3, 2)
CHUNK = 256


def nt(left, right):
    return lax.dot_general(left, right, (((1,), (1,)), ((), ())), preferred_element_type=F32)


def iota(shape, dim):
    return lax.broadcasted_iota(jnp.int32, shape, dim)


def ones_where(condition):
    return jnp.where(condition, 1.0, 0.0).astype(BF16)


def cols(part):
    return pl.ds(PARTS[part][0], PARTS[part][1])


def turn_matrix(forward):
    row = iota((ROWS, ROWS), 0)
    if forward:
        source = ((row >> 2) & 3) * 64 + (row >> 6) * 16 + ((row >> 4) & 3) * 4 + (row & 3)
    else:
        source = ((row >> 4) & 3) * 64 + ((row >> 2) & 3) * 16 + (row >> 6) * 4 + (row & 3)
    return ones_where(source == iota((ROWS, ROWS), 1))


def kernel(
    x_ref,
    routes_ref,
    gate_ref,
    wg_hbm,
    wu_hbm,
    wd_hbm,
    sums,
    mid_ref,
    back_ref,
    home_ref,
    lines,
    tables,
    packed,
    landed,
    hidden,
    turned,
    mixes,
    mixed,
    wg,
    wu,
    wd,
    sem_send,
    sem_recv,
    end_send,
    end_recv,
    tab_send,
    tab_recv,
    w_send,
    w_recv,
    w_local,
    own_sem,
    load_sem,
    x_sem,
):
    row = lax.axis_index("expert")
    at = {"y": lax.axis_index("dp"), "x": row // 8, "z": (row // 2) % 4}
    core = row % 2

    def device(where, which):
        return (where["y"], (where["x"] * 4 + where["z"]) * 2 + which)

    def peer(axis, shift):
        where = dict(at)
        where[axis] = (at[axis] + shift) % SIDE
        return device(where, core)

    partner = device(at, 1 - core)

    barrier = pltpu.get_barrier_semaphore()
    for step in (2, 1, 3):
        for axis in "yxz":
            pl.semaphore_signal(barrier, inc=1, device_id=peer(axis, step), device_id_type=MESH)
    pl.semaphore_signal(barrier, inc=1, device_id=partner, device_id_type=MESH)

    own_rows = pltpu.make_async_copy(x_ref, lines.at[pl.ds(0, TOK)], x_sem.at[0])
    own_rows.start()
    own_weights = [
        pltpu.make_async_copy(src.at[0], dst.at[0], w_local.at[index])
        for index, (src, dst) in enumerate(((wg_hbm, wg), (wu_hbm, wu), (wd_hbm, wd)))
    ]

    quant = gate_ref[...].astype(F32)
    weight = quant / jnp.sum(quant, axis=0, keepdims=True)
    named = jnp.zeros((EXPERTS, TOK), F32)
    share = jnp.zeros((EXPERTS, TOK), F32)
    for k in range(TOP):
        hit = routes_ref[k : k + 1, :] == iota((EXPERTS, TOK), 0)
        named = named + jnp.where(hit, 1.0, 0.0)
        share = share + jnp.where(hit, weight[k : k + 1, :], 0.0)
    earlier = ones_where(iota((TOK, TOK), 0) < iota((TOK, TOK), 1))
    before = jnp.dot(named.astype(BF16), earlier, preferred_element_type=F32)
    slots = jnp.where(named > 0.5, before, -1.0)
    own_table = jnp.concatenate([slots, share], axis=0).T.astype(BF16)
    for part in range(3):
        tables[part, 0:TOK, :] = own_table

    pl.semaphore_wait(barrier, 10)

    def phase0(part, step):
        return pltpu.make_async_remote_copy(
            src_ref=x_ref.at[:, cols(part)],
            dst_ref=lines.at[pl.ds(step * TOK, TOK), cols(part)],
            send_sem=end_send.at[0, part, step],
            recv_sem=end_recv.at[0, part, step],
            device_id=peer(ORDERS[part][0], -step),
            device_id_type=MESH,
        )

    def table_copy(part, step):
        return pltpu.make_async_remote_copy(
            src_ref=tables.at[part, pl.ds(0, TOK)],
            dst_ref=tables.at[part, pl.ds(step * TOK, TOK)],
            send_sem=tab_send.at[part, step],
            recv_sem=tab_recv.at[part, step],
            device_id=peer(ORDERS[part][0], -step),
            device_id_type=MESH,
        )

    for step in STEPS:
        for part in range(3):
            table_copy(part, step).start()
    for step in STEPS:
        for part in range(3):
            phase0(part, step).start()

    other_weights = [
        pltpu.make_async_remote_copy(
            src_ref=src.at[0],
            dst_ref=dst.at[1],
            send_sem=w_send.at[index],
            recv_sem=w_recv.at[index],
            device_id=partner,
            device_id_type=MESH,
        )
        for index, (src, dst) in enumerate(((wg_hbm, wg), (wu_hbm, wu), (wd_hbm, wd)))
    ]
    for copy in own_weights + other_weights:
        copy.start()

    def chosen(part):
        index = iota((ROWS, EXPERTS), 0)
        a, b, c = (at[axis] for axis in ORDERS[part])
        where = dict(zip(ORDERS[part], (a, (b - (index >> 6)) & 3, (c - ((index >> 4) & 3)) & 3)))
        expert = where["y"] * 16 + where["x"] * 4 + where["z"]
        return ones_where(expert == iota((ROWS, EXPERTS), 1))

    def sends(phase, group, part, step, src, dst, target):
        return pltpu.make_async_remote_copy(
            src_ref=src,
            dst_ref=dst,
            send_sem=sem_send.at[phase, group, part, step],
            recv_sem=sem_recv.at[phase, group, part, step],
            device_id=target,
            device_id_type=MESH,
        )

    def hop(phase, group, part, step):
        order = ORDERS[part]
        here = cols(part)
        if phase == 0:
            src, dst = packed.at[group, step, :, :, here], mid_ref.at[group, :, step, :, here]
            target = (order[1], -step)
        elif phase == 1:
            src, dst = mid_ref.at[group, step, :, :, here], landed.at[group, step, :, :, here]
            target = (order[2], -step)
        elif phase == 2:
            src, dst = landed.at[group, step, :, :, here], back_ref.at[group, :, step, :, here]
            target = (order[2], step)
        else:
            src, dst = back_ref.at[group, step, :, :, here], home_ref.at[group, step, :, :, here]
            target = (order[1], step)
        if step == 0:
            if phase == 3:
                dst = packed.at[group, 0, :, :, here]
            return pltpu.make_async_copy(src, dst, own_sem.at[phase, group, part])
        return sends(phase, group, part, step, src, dst, peer(*target))

    def start(phase, group, part):
        for step in STEPS + (0,):
            hop(phase, group, part, step).start()

    def finish(phase, group, part):
        for step in (0,) + STEPS:
            hop(phase, group, part, step).wait()

    def start_all(phase, group):
        for step in STEPS + (0,):
            for part in range(3):
                hop(phase, group, part, step).start()

    def finish_all(phase, group):
        for part in range(3):
            finish(phase, group, part)

    def gather(group, part):
        first, size = PARTS[part]
        found = nt(chosen(part), tables[part, :, 0:EXPERTS])
        row = iota((ROWS, SIDE * TOK), 0)
        slot = (row & 3) + group * SLOTS
        holder = iota((ROWS, SIDE * TOK), 1) >> 6
        pick = ones_where((found == slot.astype(F32)) & (holder == ((row >> 2) & 3)))
        rows = jnp.dot(pick, lines[:, first : first + size], preferred_element_type=F32)
        packed[group, :, :, :, first : first + size] = rows.astype(BF16).reshape(SIDE, SIDE, BLOCK, size)

    def mix_tables(part):
        select = chosen(part)
        found = nt(tables[part, :, 0:EXPERTS], select)
        scale = nt(tables[part, :, EXPERTS : 2 * EXPERTS], select)
        col = iota((SIDE * TOK, ROWS), 1)
        mine = (iota((SIDE * TOK, ROWS), 0) >> 6) == ((col >> 2) & 3)
        for group in range(GROUPS):
            slot = (col & 3) + group * SLOTS
            mixes[group, part] = jnp.where((found == slot.astype(F32)) & mine, scale, 0.0).astype(BF16)

    own_rows.wait()
    for part in range(3):
        for step in STEPS:
            table_copy(part, step).wait()
    for part in range(3):
        for step in STEPS:
            phase0(part, step).wait()
        gather(0, part)
        start(0, 0, part)
    for part in range(3):
        gather(1, part)
        start(0, 1, part)
    for part in range(3):
        gather(2, part)
    for part in range(3):
        finish(0, 0, part)
        start(1, 0, part)
    for part in range(3):
        start(0, 2, part)
    for part in range(3):
        mix_tables(part)
    for part in range(3):
        finish(0, 1, part)
        start(1, 1, part)

    def arrange(group):
        for part in range(3):
            first, size = PARTS[part]
            rows = landed[group, :, :, :, first : first + size]
            if part:
                rows = rows.reshape(ROWS, size)
                rows = jnp.dot(turn_matrix(part == 1), rows, preferred_element_type=F32)
                rows = rows.astype(BF16).reshape(SIDE, SIDE, BLOCK, size)
            packed[group, :, :, :, first : first + size] = rows

    def inner(group):
        @pl.loop(0, 2 * HALF // CHUNK)
        def _(index):
            side = index // (HALF // CHUNK)
            these = pl.ds(pl.multiple_of((index % (HALF // CHUNK)) * CHUNK, CHUNK), CHUNK)
            those = pl.ds(pl.multiple_of(index * CHUNK, CHUNK), CHUNK)
            rows = packed[group].reshape(ROWS, WIDTH)
            gate = jnp.dot(rows, wg[side, :, these], preferred_element_type=F32)
            upper = jnp.dot(rows, wu[side, :, these], preferred_element_type=F32)
            hidden[:, those] = (gate / (1.0 + jnp.exp(-gate)) * upper).astype(BF16)

    def outer(group, part):
        first, size = PARTS[part]
        source = hidden
        if part:
            turned[...] = jnp.dot(
                turn_matrix(part == 2), hidden[...], preferred_element_type=F32
            ).astype(BF16)
            source = turned
        for begin in range(first, first + size, CHUNK):
            end = min(begin + CHUNK, first + size)
            total = jnp.dot(source[:, :HALF], wd[0, :, begin:end], preferred_element_type=F32)
            total = total + jnp.dot(source[:, HALF:], wd[1, :, begin:end], preferred_element_type=F32)
            landed[group, :, :, :, begin:end] = total.astype(BF16).reshape(SIDE, SIDE, BLOCK, end - begin)

    for copy in own_weights + other_weights:
        copy.wait()

    for group in range(GROUPS):
        finish_all(1, group)
        arrange(group)
        inner(group)
        if group == 0:
            for part in range(3):
                finish(0, 2, part)
                start(1, 2, part)
        else:
            for part in range(3):
                finish(2, group - 1, part)
                start(3, group - 1, part)
        for part in range(3):
            outer(group, part)
            start(2, group, part)

    def load(group, part, step):
        return pltpu.make_async_copy(
            home_ref.at[group, step, :, :, cols(part)],
            packed.at[group, step, :, :, cols(part)],
            load_sem.at[group, part, step],
        )

    def bring(group, part):
        finish(3, group, part)
        for step in STEPS:
            load(group, part, step).start()

    def mix(group, part):
        first, size = PARTS[part]
        for step in STEPS:
            load(group, part, step).wait()
        rows = packed[group, :, :, :, first : first + size].reshape(ROWS, size)
        total = jnp.dot(mixes[group, part], rows, preferred_element_type=F32)
        if group:
            total = total + mixed[:, first : first + size]
        if group == GROUPS - 1:
            lines[:, first : first + size] = total.astype(BF16)
        else:
            mixed[:, first : first + size] = total

    def phase5(part, step):
        src = lines.at[pl.ds(step * TOK, TOK), cols(part)]
        dst = sums.at[step, :, cols(part)]
        if step == 0:
            return pltpu.make_async_copy(src, dst, x_sem.at[1 + part])
        return pltpu.make_async_remote_copy(
            src_ref=src,
            dst_ref=dst,
            send_sem=end_send.at[1, part, step],
            recv_sem=end_recv.at[1, part, step],
            device_id=peer(ORDERS[part][0], step),
            device_id_type=MESH,
        )

    for part in range(3):
        bring(0, part)
    for part in range(3):
        mix(0, part)
    for part in range(3):
        finish(2, 2, part)
        start(3, 2, part)
    for part in range(3):
        bring(1, part)
    for part in range(3):
        mix(1, part)
    for part in range(3):
        bring(2, part)
        mix(2, part)
        for step in STEPS + (0,):
            phase5(part, step).start()
    for part in range(3):
        for step in STEPS + (0,):
            phase5(part, step).wait()


def on_device(tokens, routes, gate_fixed, w_gate, w_up, w_down):
    big = jax.ShapeDtypeStruct((GROUPS, SIDE, SIDE, BLOCK, WIDTH), BF16)
    vmem = pl.BlockSpec(memory_space=pltpu.VMEM)
    hbm = pl.BlockSpec(memory_space=pltpu.HBM)
    dma = pltpu.SemaphoreType.DMA
    sums, _, _, _ = pl.pallas_call(
        kernel,
        out_shape=(jax.ShapeDtypeStruct((SIDE, TOK, WIDTH), BF16), big, big, big),
        in_specs=[hbm, vmem, vmem, hbm, hbm, hbm],
        out_specs=(hbm, hbm, hbm, hbm),
        scratch_shapes=[
            pltpu.VMEM((SIDE * TOK, WIDTH), BF16),
            pltpu.VMEM((3, SIDE * TOK, 2 * EXPERTS), BF16),
            pltpu.VMEM((GROUPS, SIDE, SIDE, BLOCK, WIDTH), BF16),
            pltpu.VMEM((GROUPS, SIDE, SIDE, BLOCK, WIDTH), BF16),
            pltpu.VMEM((ROWS, 2 * HALF), BF16),
            pltpu.VMEM((ROWS, 2 * HALF), BF16),
            pltpu.VMEM((GROUPS, 3, SIDE * TOK, ROWS), BF16),
            pltpu.VMEM((SIDE * TOK, WIDTH), F32),
            pltpu.VMEM((2, WIDTH, HALF), BF16),
            pltpu.VMEM((2, WIDTH, HALF), BF16),
            pltpu.VMEM((2, HALF, WIDTH), BF16),
            dma((4, GROUPS, 3, SIDE)),
            dma((4, GROUPS, 3, SIDE)),
            dma((2, 3, SIDE)),
            dma((2, 3, SIDE)),
            dma((3, SIDE)),
            dma((3, SIDE)),
            dma((3,)),
            dma((3,)),
            dma((3,)),
            dma((4, GROUPS, 3)),
            dma((GROUPS, 3, SIDE)),
            dma((4,)),
        ],
        compiler_params=pltpu.CompilerParams(
            collective_id=0, has_side_effects=True, vmem_limit_bytes=67043328
        ),
        name="moe",
    )(tokens, routes.T, gate_fixed.T, w_gate, w_up, w_down)
    return jnp.sum(sums.astype(F32), axis=0).astype(BF16)


def solution(mesh):
    split = P(("dp", "expert"), None)
    placed = (split, split, split) + (P(("dp", "expert"), None, None),) * 3
    return jax.shard_map(on_device, mesh=mesh, in_specs=placed, out_specs=split, check_vma=False)
```

```python
import jax
import jax.numpy as jnp
from jax import lax
from jax.experimental import pallas as pl
from jax.experimental.pallas import tpu as pltpu
from jax.sharding import PartitionSpec as P

MESH = pl.DeviceIdType.MESH
F32 = jnp.float32
BF16 = jnp.bfloat16

SIDE = 4
TOK = 64
TOP = 8
EXPERTS = 64
WIDTH = 4096
HALF = 768
GROUPS = 3
SLOTS = 4
BLOCK = SIDE * SLOTS
ROWS = SIDE * SIDE * BLOCK

PARTS = ((0, 1408), (1408, 1408), (2816, 1280))
BACK_PARTS = ((0, 1280), (1280, 1408), (2688, 1408))
ORDERS = ("yxz", "xzy", "zyx")
STEPS = (1, 3, 2)
CHUNK = 256


def nt(left, right):
    return lax.dot_general(left, right, (((1,), (1,)), ((), ())), preferred_element_type=F32)


def iota(shape, dim):
    return lax.broadcasted_iota(jnp.int32, shape, dim)


def ones_where(condition):
    return jnp.where(condition, 1.0, 0.0).astype(BF16)


def cols(part):
    return pl.ds(PARTS[part][0], PARTS[part][1])


def back_cols(part):
    return pl.ds(BACK_PARTS[part][0], BACK_PARTS[part][1])


RELAYED = {1: 0, 3: 1}


def half_cols(parts, part, half):
    first, size = parts[part]
    cut = 640
    return pl.ds(first + half * cut, size - cut if half else cut)


def turn_matrix(forward):
    row = iota((ROWS, ROWS), 0)
    if forward:
        source = ((row >> 2) & 3) * 64 + (row >> 6) * 16 + ((row >> 4) & 3) * 4 + (row & 3)
    else:
        source = ((row >> 4) & 3) * 64 + ((row >> 2) & 3) * 16 + (row >> 6) * 4 + (row & 3)
    return ones_where(source == iota((ROWS, ROWS), 1))


def kernel(
    x_ref,
    routes_ref,
    gate_ref,
    wg_hbm,
    wu_hbm,
    wd_hbm,
    sums,
    mid_ref,
    back_ref,
    home_ref,
    lines,
    passing,
    tables,
    packed,
    landed,
    hidden,
    turned,
    mixes,
    mixed,
    wg,
    wu,
    wd,
    sem_send,
    sem_recv,
    start_send,
    start_recv,
    end_send,
    end_recv,
    tab_send,
    tab_recv,
    w_send,
    w_recv,
    w_local,
    own_sem,
    load_sem,
    x_sem,
):
    row = lax.axis_index("expert")
    at = {"y": lax.axis_index("dp"), "x": row // 8, "z": (row // 2) % 4}
    core = row % 2

    def device(where, which):
        return (where["y"], (where["x"] * 4 + where["z"]) * 2 + which)

    def peer(axis, shift):
        where = dict(at)
        where[axis] = (at[axis] + shift) % SIDE
        return device(where, core)

    partner = device(at, 1 - core)

    barrier = pltpu.get_barrier_semaphore()
    for step in (1, 3):
        for axis in "yxz":
            pl.semaphore_signal(barrier, inc=1, device_id=peer(axis, step), device_id_type=MESH)
    pl.semaphore_signal(barrier, inc=1, device_id=partner, device_id_type=MESH)

    own_rows = pltpu.make_async_copy(x_ref, lines.at[pl.ds(0, TOK)], x_sem.at[0])
    own_rows.start()
    own_weights = [
        pltpu.make_async_copy(src.at[0], dst.at[0], w_local.at[index])
        for index, (src, dst) in enumerate(((wg_hbm, wg), (wu_hbm, wu), (wd_hbm, wd)))
    ]

    quant = gate_ref[...].astype(F32)
    weight = quant / jnp.sum(quant, axis=0, keepdims=True)
    named = jnp.zeros((EXPERTS, TOK), F32)
    share = jnp.zeros((EXPERTS, TOK), F32)
    for k in range(TOP):
        hit = routes_ref[k : k + 1, :] == iota((EXPERTS, TOK), 0)
        named = named + jnp.where(hit, 1.0, 0.0)
        share = share + jnp.where(hit, weight[k : k + 1, :], 0.0)
    earlier = ones_where(iota((TOK, TOK), 0) < iota((TOK, TOK), 1))
    before = jnp.dot(named.astype(BF16), earlier, preferred_element_type=F32)
    slots = jnp.where(named > 0.5, before, -1.0)
    own_table = jnp.concatenate([slots, share], axis=0).T.astype(BF16)
    for part in range(3):
        tables[part, 0:TOK, :] = own_table

    pl.semaphore_wait(barrier, 7)

    def phase0(part, step, half):
        here = half_cols(PARTS, part, half)
        return pltpu.make_async_remote_copy(
            src_ref=x_ref.at[:, here],
            dst_ref=lines.at[pl.ds(step * TOK, TOK), here],
            send_sem=start_send.at[half, part, step],
            recv_sem=start_recv.at[half, part, step],
            device_id=peer(ORDERS[part][0], -step),
            device_id_type=MESH,
        )

    def relay0(part, step):
        here = half_cols(PARTS, part, RELAYED[step])
        return pltpu.make_async_remote_copy(
            src_ref=lines.at[pl.ds(step * TOK, TOK), here],
            dst_ref=lines.at[pl.ds(2 * TOK, TOK), here],
            send_sem=start_send.at[2, part, step],
            recv_sem=start_recv.at[2, part, step],
            device_id=peer(ORDERS[part][0], -step),
            device_id_type=MESH,
        )

    def table_copy(part, step):
        origin = 1 if step == 2 else 0
        return pltpu.make_async_remote_copy(
            src_ref=tables.at[part, pl.ds(origin * TOK, TOK)],
            dst_ref=tables.at[part, pl.ds(step * TOK, TOK)],
            send_sem=tab_send.at[part, step],
            recv_sem=tab_recv.at[part, step],
            device_id=peer(ORDERS[part][0], origin - step),
            device_id_type=MESH,
        )

    for step in (1, 3):
        for part in range(3):
            table_copy(part, step).start()
    for first_half in (True, False):
        for step in (1, 3):
            for part in range(3):
                phase0(part, step, RELAYED[step] if first_half else 1 - RELAYED[step]).start()

    other_weights = [
        pltpu.make_async_remote_copy(
            src_ref=src.at[0],
            dst_ref=dst.at[1],
            send_sem=w_send.at[index],
            recv_sem=w_recv.at[index],
            device_id=partner,
            device_id_type=MESH,
        )
        for index, (src, dst) in enumerate(((wg_hbm, wg), (wu_hbm, wu), (wd_hbm, wd)))
    ]
    for copy in own_weights + other_weights:
        copy.start()

    def chosen(part):
        index = iota((ROWS, EXPERTS), 0)
        a, b, c = (at[axis] for axis in ORDERS[part])
        where = dict(zip(ORDERS[part], (a, (b - (index >> 6)) & 3, (c - ((index >> 4) & 3)) & 3)))
        expert = where["y"] * 16 + where["x"] * 4 + where["z"]
        return ones_where(expert == iota((ROWS, EXPERTS), 1))

    def sends(phase, group, part, step, src, dst, target):
        return pltpu.make_async_remote_copy(
            src_ref=src,
            dst_ref=dst,
            send_sem=sem_send.at[phase, group, part, step],
            recv_sem=sem_recv.at[phase, group, part, step],
            device_id=target,
            device_id_type=MESH,
        )

    def hop(phase, group, part, step):
        order = ORDERS[part]
        here = cols(part)
        if phase == 0:
            src, dst = packed.at[group, step, :, :, here], mid_ref.at[group, :, step, :, here]
            target = (order[1], -step)
        elif phase == 1:
            src, dst = mid_ref.at[group, step, :, :, here], landed.at[group, step, :, :, here]
            target = (order[2], -step)
        elif phase == 2:
            here = back_cols(part)
            src, dst = landed.at[group, step, :, :, here], back_ref.at[group, :, step, :, here]
            target = (order[2], step)
        else:
            here = back_cols(part)
            src, dst = back_ref.at[group, step, :, :, here], home_ref.at[group, step, :, :, here]
            target = (order[1], step)
        if step == 0:
            if phase == 3:
                dst = packed.at[group, 0, :, :, here]
            return pltpu.make_async_copy(src, dst, own_sem.at[phase, group, part])
        return sends(phase, group, part, step, src, dst, peer(*target))

    def start(phase, group, part):
        for step in STEPS + (0,):
            hop(phase, group, part, step).start()

    def finish(phase, group, part):
        for step in (0,) + STEPS:
            hop(phase, group, part, step).wait()

    def start_all(phase, group):
        for step in STEPS + (0,):
            for part in range(3):
                hop(phase, group, part, step).start()

    def finish_all(phase, group):
        for part in range(3):
            finish(phase, group, part)

    def gather(group, part):
        first, size = PARTS[part]
        found = nt(chosen(part), tables[part, :, 0:EXPERTS])
        row = iota((ROWS, SIDE * TOK), 0)
        slot = (row & 3) + group * SLOTS
        holder = iota((ROWS, SIDE * TOK), 1) >> 6
        pick = ones_where((found == slot.astype(F32)) & (holder == ((row >> 2) & 3)))
        rows = jnp.dot(pick, lines[:, first : first + size], preferred_element_type=F32)
        packed[group, :, :, :, first : first + size] = rows.astype(BF16).reshape(SIDE, SIDE, BLOCK, size)

    def mix_tables(part):
        select = chosen(part)
        found = nt(tables[part, :, 0:EXPERTS], select)
        scale = nt(tables[part, :, EXPERTS : 2 * EXPERTS], select)
        col = iota((SIDE * TOK, ROWS), 1)
        mine = (iota((SIDE * TOK, ROWS), 0) >> 6) == ((col >> 2) & 3)
        for group in range(GROUPS):
            slot = (col & 3) + group * SLOTS
            mixes[group, part] = jnp.where((found == slot.astype(F32)) & mine, scale, 0.0).astype(BF16)

    for part in range(3):
        table_copy(part, 1).wait_recv()
        table_copy(part, 2).start()
    for part in range(3):
        for step in (1, 3):
            phase0(part, step, RELAYED[step]).wait_recv()
            relay0(part, step).start()
    own_rows.wait()
    for part in range(3):
        table_copy(part, 3).wait_recv()
        table_copy(part, 2).wait_recv()
    for part in range(3):
        for step in (1, 3):
            phase0(part, step, 1 - RELAYED[step]).wait_recv()
        for step in (1, 3):
            relay0(part, step).wait_recv()
        gather(0, part)
        start(0, 0, part)
    for part in range(3):
        gather(1, part)
        start(0, 1, part)
    for part in range(3):
        gather(2, part)
    for part in range(3):
        finish(0, 0, part)
        start(1, 0, part)
    for part in range(3):
        start(0, 2, part)
    for part in range(3):
        mix_tables(part)
    for part in range(3):
        for step in STEPS:
            table_copy(part, step).wait_send()
        for step in (1, 3):
            phase0(part, step, 0).wait_send()
            phase0(part, step, 1).wait_send()
            relay0(part, step).wait_send()
    for part in range(3):
        finish(0, 1, part)
        start(1, 1, part)

    def arrange(group):
        for part in range(3):
            first, size = PARTS[part]
            rows = landed[group, :, :, :, first : first + size]
            if part:
                rows = rows.reshape(ROWS, size)
                rows = jnp.dot(turn_matrix(part == 1), rows, preferred_element_type=F32)
                rows = rows.astype(BF16).reshape(SIDE, SIDE, BLOCK, size)
            packed[group, :, :, :, first : first + size] = rows

    def inner(group):
        @pl.loop(0, 2 * HALF // CHUNK)
        def _(index):
            side = index // (HALF // CHUNK)
            these = pl.ds(pl.multiple_of((index % (HALF // CHUNK)) * CHUNK, CHUNK), CHUNK)
            those = pl.ds(pl.multiple_of(index * CHUNK, CHUNK), CHUNK)
            rows = packed[group].reshape(ROWS, WIDTH)
            gate = jnp.dot(rows, wg[side, :, these], preferred_element_type=F32)
            upper = jnp.dot(rows, wu[side, :, these], preferred_element_type=F32)
            hidden[:, those] = (gate / (1.0 + jnp.exp(-gate)) * upper).astype(BF16)

    def outer(group, part):
        first, size = BACK_PARTS[part]
        source = hidden
        if part:
            turned[...] = jnp.dot(
                turn_matrix(part == 2), hidden[...], preferred_element_type=F32
            ).astype(BF16)
            source = turned
        for begin in range(first, first + size, CHUNK):
            end = min(begin + CHUNK, first + size)
            total = jnp.dot(source[:, :HALF], wd[0, :, begin:end], preferred_element_type=F32)
            total = total + jnp.dot(source[:, HALF:], wd[1, :, begin:end], preferred_element_type=F32)
            landed[group, :, :, :, begin:end] = total.astype(BF16).reshape(SIDE, SIDE, BLOCK, end - begin)

    for copy in own_weights + other_weights:
        copy.wait()

    for group in range(GROUPS):
        finish_all(1, group)
        arrange(group)
        inner(group)
        if group == 0:
            for part in range(3):
                finish(0, 2, part)
                start(1, 2, part)
        for part in range(3):
            outer(group, part)
            start(2, group, part)
        if group:
            for part in range(3):
                finish(2, group - 1, part)
                start(3, group - 1, part)

    def load(group, part, step):
        return pltpu.make_async_copy(
            home_ref.at[group, step, :, :, back_cols(part)],
            packed.at[group, step, :, :, back_cols(part)],
            load_sem.at[group, part, step],
        )

    def bring(group, part):
        finish(3, group, part)
        for step in STEPS:
            load(group, part, step).start()

    def mix(group, part):
        here = back_cols(part)
        for step in STEPS:
            load(group, part, step).wait()
        rows = packed[group, :, :, :, here].reshape(ROWS, BACK_PARTS[part][1])
        total = jnp.dot(mixes[group, part], rows, preferred_element_type=F32)
        if group:
            total = total + mixed[:, here]
        mixed[:, here] = total
        if group == GROUPS - 1:
            lines[:, here] = total.astype(BF16)

    def relay5(part, step):
        here = half_cols(BACK_PARTS, part, RELAYED[step])
        return pltpu.make_async_remote_copy(
            src_ref=lines.at[pl.ds(2 * TOK, TOK), here],
            dst_ref=passing.at[:, here],
            send_sem=end_send.at[2, part, step],
            recv_sem=end_recv.at[2, part, step],
            device_id=peer(ORDERS[part][0], step),
            device_id_type=MESH,
        )

    def phase5(part, step, half):
        here = half_cols(BACK_PARTS, part, half)
        return pltpu.make_async_remote_copy(
            src_ref=lines.at[pl.ds(step * TOK, TOK), here],
            dst_ref=sums.at[(step + 1) // 2, :, here],
            send_sem=end_send.at[half, part, step],
            recv_sem=end_recv.at[half, part, step],
            device_id=peer(ORDERS[part][0], step),
            device_id_type=MESH,
        )

    def own5(part):
        here = back_cols(part)
        return pltpu.make_async_copy(lines.at[pl.ds(0, TOK), here], sums.at[0, :, here], x_sem.at[1 + part])

    for part in range(3):
        bring(0, part)
    for part in range(3):
        mix(0, part)
    for part in range(3):
        finish(2, 2, part)
        start(3, 2, part)
    for part in range(3):
        bring(1, part)
    for part in range(3):
        mix(1, part)
    for part in range(3):
        bring(2, part)
        mix(2, part)
        for step in (1, 3):
            relay5(part, step).start()
        for step in (1, 3):
            phase5(part, step, 1 - RELAYED[step]).start()
        own5(part).start()
    for part in range(3):
        for step in (1, 3):
            here = half_cols(BACK_PARTS, part, RELAYED[step])
            these = slice(step * TOK, (step + 1) * TOK)
            relay5(part, step).wait_recv()
            lines[these, here] = (mixed[these, here] + passing[:, here].astype(F32)).astype(BF16)
            phase5(part, step, RELAYED[step]).start()
    for part in range(3):
        own5(part).wait()
        for step in (1, 3):
            relay5(part, step).wait_send()
            phase5(part, step, 0).wait()
            phase5(part, step, 1).wait()


def on_device(tokens, routes, gate_fixed, w_gate, w_up, w_down):
    big = jax.ShapeDtypeStruct((GROUPS, SIDE, SIDE, BLOCK, WIDTH), BF16)
    vmem = pl.BlockSpec(memory_space=pltpu.VMEM)
    hbm = pl.BlockSpec(memory_space=pltpu.HBM)
    dma = pltpu.SemaphoreType.DMA
    sums, _, _, _ = pl.pallas_call(
        kernel,
        out_shape=(jax.ShapeDtypeStruct((3, TOK, WIDTH), BF16), big, big, big),
        in_specs=[hbm, vmem, vmem, hbm, hbm, hbm],
        out_specs=(hbm, hbm, hbm, hbm),
        scratch_shapes=[
            pltpu.VMEM((SIDE * TOK, WIDTH), BF16),
            pltpu.VMEM((TOK, WIDTH), BF16),
            pltpu.VMEM((3, SIDE * TOK, 2 * EXPERTS), BF16),
            pltpu.VMEM((GROUPS, SIDE, SIDE, BLOCK, WIDTH), BF16),
            pltpu.VMEM((GROUPS, SIDE, SIDE, BLOCK, WIDTH), BF16),
            pltpu.VMEM((ROWS, 2 * HALF), BF16),
            pltpu.VMEM((ROWS, 2 * HALF), BF16),
            pltpu.VMEM((GROUPS, 3, SIDE * TOK, ROWS), BF16),
            pltpu.VMEM((SIDE * TOK, WIDTH), F32),
            pltpu.VMEM((2, WIDTH, HALF), BF16),
            pltpu.VMEM((2, WIDTH, HALF), BF16),
            pltpu.VMEM((2, HALF, WIDTH), BF16),
            dma((4, GROUPS, 3, SIDE)),
            dma((4, GROUPS, 3, SIDE)),
            dma((3, 3, SIDE)),
            dma((3, 3, SIDE)),
            dma((3, 3, SIDE)),
            dma((3, 3, SIDE)),
            dma((3, SIDE)),
            dma((3, SIDE)),
            dma((3,)),
            dma((3,)),
            dma((3,)),
            dma((4, GROUPS, 3)),
            dma((GROUPS, 3, SIDE)),
            dma((4,)),
        ],
        compiler_params=pltpu.CompilerParams(
            collective_id=0, has_side_effects=True, vmem_limit_bytes=67043328
        ),
        name="moe",
    )(tokens, routes.T, gate_fixed.T, w_gate, w_up, w_down)
    return jnp.sum(sums.astype(F32), axis=0).astype(BF16)


def solution(mesh):
    split = P(("dp", "expert"), None)
    placed = (split, split, split) + (P(("dp", "expert"), None, None),) * 3
    return jax.shard_map(on_device, mesh=mesh, in_specs=placed, out_specs=split, check_vma=False)
```

```python
import jax
import jax.numpy as jnp
from jax import lax
from jax.experimental import pallas as pl
from jax.experimental.pallas import tpu as pltpu
from jax.sharding import PartitionSpec as P

MESH = pl.DeviceIdType.MESH
F32 = jnp.float32
BF16 = jnp.bfloat16

SIDE = 4
TOK = 64
TOP = 8
EXPERTS = 64
WIDTH = 4096
HALF = 768
GROUPS = 3
SLOTS = 4
BLOCK = SIDE * SLOTS
ROWS = SIDE * SIDE * BLOCK

PARTS = ((0, 1408), (1408, 1408), (2816, 1280))
BACK_PARTS = ((0, 1280), (1280, 1408), (2688, 1408))
ORDERS = ("yxz", "xzy", "zyx")
STEPS = (1, 3, 2)
CHUNK = 256


def nt(left, right):
    return lax.dot_general(left, right, (((1,), (1,)), ((), ())), preferred_element_type=F32)


def iota(shape, dim):
    return lax.broadcasted_iota(jnp.int32, shape, dim)


def ones_where(condition):
    return jnp.where(condition, 1.0, 0.0).astype(BF16)


def cols(part):
    return pl.ds(PARTS[part][0], PARTS[part][1])


def back_cols(part):
    return pl.ds(BACK_PARTS[part][0], BACK_PARTS[part][1])


RELAYED = {1: 0, 3: 1}


def stretch(parts, part, rest):
    first, size = parts[part]
    cut = 768 if parts is PARTS else size - 384
    return (first + cut, size - cut) if rest else (first, cut)


def stretch_cols(parts, part, rest):
    return pl.ds(*stretch(parts, part, rest))


def half_cols(parts, part, rest, half):
    first, size = stretch(parts, part, rest)
    cut = (size // 2 + 127) // 128 * 128
    return pl.ds(first + cut, size - cut) if half else pl.ds(first, cut)


def turn_matrix(forward):
    row = iota((ROWS, ROWS), 0)
    if forward:
        source = ((row >> 2) & 3) * 64 + (row >> 6) * 16 + ((row >> 4) & 3) * 4 + (row & 3)
    else:
        source = ((row >> 4) & 3) * 64 + ((row >> 2) & 3) * 16 + (row >> 6) * 4 + (row & 3)
    return ones_where(source == iota((ROWS, ROWS), 1))


def kernel(
    x_ref,
    routes_hbm,
    gate_hbm,
    wg_hbm,
    wu_hbm,
    wd_hbm,
    sums,
    mid_ref,
    back_ref,
    home_ref,
    routes_ref,
    gate_ref,
    lines,
    passing,
    last,
    tables,
    packed,
    landed,
    hidden,
    turned,
    mixes,
    mixed,
    wg,
    wu,
    wd,
    hop_send,
    hop_recv,
    start_send,
    first_recv,
    start_recv,
    pass_recv,
    end_sem,
    tab_sem,
    w_send,
    w_recv,
    w_local,
    own_sem,
    load_sem,
    x_sem,
):
    row = lax.axis_index("expert")
    at = {"y": lax.axis_index("dp"), "x": row // 8, "z": (row // 2) % 4}
    core = row % 2

    def device(where, which):
        return (where["y"], (where["x"] * 4 + where["z"]) * 2 + which)

    def peer(axis, shift):
        where = dict(at)
        where[axis] = (at[axis] + shift) % SIDE
        return device(where, core)

    partner = device(at, 1 - core)

    barrier = pltpu.get_barrier_semaphore()
    for step in (1, 3):
        for axis in "yxz":
            pl.semaphore_signal(barrier, inc=1, device_id=peer(axis, step), device_id_type=MESH)
    pl.semaphore_signal(barrier, inc=1, device_id=partner, device_id_type=MESH)

    def wait_bytes(ref, sem):
        pltpu.make_async_copy(ref, ref, sem).wait()

    own_rows = pltpu.make_async_copy(x_ref, lines.at[pl.ds(0, TOK)], x_sem.at[0])
    own_choices = [
        pltpu.make_async_copy(routes_hbm, routes_ref, x_sem.at[1]),
        pltpu.make_async_copy(gate_hbm, gate_ref, x_sem.at[2]),
    ]
    for copy in own_choices + [own_rows]:
        copy.start()
    own_weights = [
        pltpu.make_async_copy(src.at[0], dst.at[0], w_local.at[index])
        for index, (src, dst) in enumerate(((wg_hbm, wg), (wu_hbm, wu), (wd_hbm, wd)))
    ]

    pl.semaphore_wait(barrier, 7)

    def phase0(part, step, rest, half):
        here = half_cols(PARTS, part, rest, half)
        return pltpu.make_async_remote_copy(
            src_ref=x_ref.at[:, here],
            dst_ref=lines.at[pl.ds(step * TOK, TOK), here],
            send_sem=start_send.at[0],
            recv_sem=first_recv.at[rest, part, step // 2] if half == RELAYED[step] else start_recv.at[rest, part],
            device_id=peer(ORDERS[part][0], -step),
            device_id_type=MESH,
        )

    def relay0(part, step, rest):
        here = half_cols(PARTS, part, rest, RELAYED[step])
        return pltpu.make_async_remote_copy(
            src_ref=lines.at[pl.ds(step * TOK, TOK), here],
            dst_ref=lines.at[pl.ds(2 * TOK, TOK), here],
            send_sem=start_send.at[0],
            recv_sem=start_recv.at[rest, part],
            device_id=peer(ORDERS[part][0], -step),
            device_id_type=MESH,
        )

    def table_copy(part, step):
        origin = 1 if step == 2 else 0
        return pltpu.make_async_remote_copy(
            src_ref=tables.at[part, pl.ds(origin * TOK, TOK)],
            dst_ref=tables.at[part, pl.ds(step * TOK, TOK)],
            send_sem=tab_sem.at[0],
            recv_sem=tab_sem.at[1 if step == 1 else 2],
            device_id=peer(ORDERS[part][0], origin - step),
            device_id_type=MESH,
        )

    def start_tokens(rest, relayed):
        for step in (1, 3):
            for part in range(3):
                phase0(part, step, rest, RELAYED[step] if relayed else 1 - RELAYED[step]).start()

    def pass_on(rest):
        for part in range(3):
            for step in (1, 3):
                phase0(part, step, rest, RELAYED[step]).wait_recv()
                relay0(part, step, rest).start()

    start_tokens(0, True)
    start_tokens(0, False)
    for copy in own_choices:
        copy.wait()

    quant = gate_ref[...].astype(F32)
    weight = quant / jnp.sum(quant, axis=0, keepdims=True)
    named = jnp.zeros((EXPERTS, TOK), F32)
    share = jnp.zeros((EXPERTS, TOK), F32)
    for k in range(TOP):
        hit = routes_ref[k : k + 1, :] == iota((EXPERTS, TOK), 0)
        named = named + jnp.where(hit, 1.0, 0.0)
        share = share + jnp.where(hit, weight[k : k + 1, :], 0.0)
    earlier = ones_where(iota((TOK, TOK), 0) < iota((TOK, TOK), 1))
    before = jnp.dot(named.astype(BF16), earlier, preferred_element_type=F32)
    slots = jnp.where(named > 0.5, before, -1.0)
    own_table = jnp.concatenate([slots, share], axis=0).T.astype(BF16)
    for part in range(3):
        tables[part, 0:TOK, :] = own_table

    for step in (1, 3):
        for part in range(3):
            table_copy(part, step).start()
    start_tokens(1, True)

    other_weights = [
        pltpu.make_async_remote_copy(
            src_ref=src.at[0],
            dst_ref=dst.at[1],
            send_sem=w_send.at[index],
            recv_sem=w_recv.at[index],
            device_id=partner,
            device_id_type=MESH,
        )
        for index, (src, dst) in enumerate(((wg_hbm, wg), (wu_hbm, wu), (wd_hbm, wd)))
    ]

    def chosen(part):
        index = iota((ROWS, EXPERTS), 0)
        a, b, c = (at[axis] for axis in ORDERS[part])
        where = dict(zip(ORDERS[part], (a, (b - (index >> 6)) & 3, (c - ((index >> 4) & 3)) & 3)))
        expert = where["y"] * 16 + where["x"] * 4 + where["z"]
        return ones_where(expert == iota((ROWS, EXPERTS), 1))

    def ends(phase, group, step, here):
        if phase == 0:
            return packed.at[group, step, :, :, here], mid_ref.at[group, :, step, :, here]
        if phase == 1:
            return mid_ref.at[group, step, :, :, here], landed.at[group, step, :, :, here]
        if phase == 2:
            return landed.at[group, step, :, :, here], back_ref.at[group, :, step, :, here]
        if group == GROUPS - 1:
            return back_ref.at[group, step, :, :, here], last.at[step, :, :, here]
        return back_ref.at[group, step, :, :, here], home_ref.at[group, step, :, :, here]

    def part_cols(phase, part, rest):
        parts = PARTS if phase < 2 else BACK_PARTS
        return pl.ds(*(parts[part] if rest is None else stretch(parts, part, rest)))

    def start(phase, group, part, rest=None):
        axis = ORDERS[part][1 if phase in (0, 3) else 2]
        for step in STEPS:
            src, dst = ends(phase, group, step, part_cols(phase, part, rest))
            pltpu.make_async_remote_copy(
                src_ref=src,
                dst_ref=dst,
                send_sem=hop_send.at[phase, group if phase == 0 else 0],
                recv_sem=hop_recv.at[phase, GROUPS if rest else group, part],
                device_id=peer(axis, step if phase > 1 else -step),
                device_id_type=MESH,
            ).start()

    def finish(phase, group, part, rest=None):
        _, dst = ends(phase, group, pl.ds(1, SIDE - 1), part_cols(phase, part, rest))
        wait_bytes(dst, hop_recv.at[phase, GROUPS if rest else group, part])

    def own_hop(phase, group):
        src, dst = ends(phase, group, 0, pl.ds(0, WIDTH))
        if phase == 3 and group < GROUPS - 1:
            dst = packed.at[group, 0]
        return pltpu.make_async_copy(src, dst, own_sem.at[phase, group])

    def start_own(phase, group):
        own_hop(phase, group).start()

    def finish_own(phase, group):
        own_hop(phase, group).wait()

    def finish_all(phase, group):
        finish_own(phase, group)
        for part in range(3):
            finish(phase, group, part)

    def gather(group, part, rest=None):
        first, size = PARTS[part] if rest is None else stretch(PARTS, part, rest)
        found = nt(chosen(part), tables[part, :, 0:EXPERTS])
        row = iota((ROWS, SIDE * TOK), 0)
        slot = (row & 3) + group * SLOTS
        holder = iota((ROWS, SIDE * TOK), 1) >> 6
        pick = ones_where((found == slot.astype(F32)) & (holder == ((row >> 2) & 3)))
        rows = jnp.dot(pick, lines[:, first : first + size], preferred_element_type=F32)
        packed[group, :, :, :, first : first + size] = rows.astype(BF16).reshape(SIDE, SIDE, BLOCK, size)

    def mix_tables(part):
        select = chosen(part)
        found = nt(tables[part, :, 0:EXPERTS], select)
        scale = nt(tables[part, :, EXPERTS : 2 * EXPERTS], select)
        col = iota((SIDE * TOK, ROWS), 1)
        mine = (iota((SIDE * TOK, ROWS), 0) >> 6) == ((col >> 2) & 3)
        for group in range(GROUPS):
            slot = (col & 3) + group * SLOTS
            mixes[group, part] = jnp.where((found == slot.astype(F32)) & mine, scale, 0.0).astype(BF16)

    wait_bytes(tables.at[:, pl.ds(0, TOK)], tab_sem.at[1])
    for part in range(3):
        table_copy(part, 2).start()
    pass_on(0)
    start_tokens(1, False)
    for copy in own_weights + other_weights:
        copy.start()
    own_rows.wait()
    pass_on(1)
    wait_bytes(tables.at[:, pl.ds(0, 2 * TOK)], tab_sem.at[2])
    for rest in range(2):
        for part in range(3):
            here = stretch_cols(PARTS, part, rest)
            wait_bytes(lines.at[pl.ds(0, 2 * TOK), here], start_recv.at[rest, part])
            gather(0, part, rest)
            start(0, 0, part, rest)
    start_own(0, 0)
    for part in range(3):
        gather(1, part)
        start(0, 1, part)
    start_own(0, 1)
    for part in range(3):
        gather(2, part)
    finish_own(0, 0)
    for part in range(3):
        finish(0, 0, part, 0)
        finish(0, 0, part, 1)
        start(1, 0, part)
    start_own(1, 0)
    for part in range(3):
        start(0, 2, part)
    start_own(0, 2)
    for part in range(3):
        mix_tables(part)
    wait_bytes(tables.at[:, pl.ds(0, 3 * TOK)], tab_sem.at[0])
    wait_bytes(lines.at[pl.ds(0, 3 * TOK)], start_send.at[0])
    finish_own(0, 1)
    for part in range(3):
        finish(0, 1, part)
        start(1, 1, part)
    start_own(1, 1)

    def arrange(group):
        for part in range(3):
            first, size = PARTS[part]
            rows = landed[group, :, :, :, first : first + size]
            if part:
                rows = rows.reshape(ROWS, size)
                rows = jnp.dot(turn_matrix(part == 1), rows, preferred_element_type=F32)
                rows = rows.astype(BF16).reshape(SIDE, SIDE, BLOCK, size)
            packed[group, :, :, :, first : first + size] = rows

    def inner(group):
        @pl.loop(0, 2 * HALF // CHUNK)
        def _(index):
            side = index // (HALF // CHUNK)
            these = pl.ds(pl.multiple_of((index % (HALF // CHUNK)) * CHUNK, CHUNK), CHUNK)
            those = pl.ds(pl.multiple_of(index * CHUNK, CHUNK), CHUNK)
            rows = packed[group].reshape(ROWS, WIDTH)
            gate = jnp.dot(rows, wg[side, :, these], preferred_element_type=F32)
            upper = jnp.dot(rows, wu[side, :, these], preferred_element_type=F32)
            hidden[:, those] = (gate / (1.0 + jnp.exp(-gate)) * upper).astype(BF16)

    def outer(group, part):
        first, size = BACK_PARTS[part]
        source = hidden
        if part:
            turned[...] = jnp.dot(
                turn_matrix(part == 2), hidden[...], preferred_element_type=F32
            ).astype(BF16)
            source = turned
        for begin in range(first, first + size, CHUNK):
            end = min(begin + CHUNK, first + size)
            total = jnp.dot(source[:, :HALF], wd[0, :, begin:end], preferred_element_type=F32)
            total = total + jnp.dot(source[:, HALF:], wd[1, :, begin:end], preferred_element_type=F32)
            landed[group, :, :, :, begin:end] = total.astype(BF16).reshape(SIDE, SIDE, BLOCK, end - begin)

    for copy in own_weights + other_weights:
        copy.wait()

    for group in range(GROUPS):
        finish_all(1, group)
        wait_bytes(packed.at[group, pl.ds(1, SIDE - 1)], hop_send.at[0, group])
        arrange(group)
        inner(group)
        if group == 0:
            finish_own(0, 2)
            for part in range(3):
                finish(0, 2, part)
                start(1, 2, part)
            start_own(1, 2)
        for part in range(3):
            outer(group, part)
            start(2, group, part)
        start_own(2, group)
        if group:
            finish_own(2, group - 1)
            for part in range(3):
                finish(2, group - 1, part)
                start(3, group - 1, part)
            start_own(3, group - 1)

    def load(group, part):
        here = back_cols(part)
        steps = pl.ds(1, SIDE - 1)
        return pltpu.make_async_copy(
            home_ref.at[group, steps, :, :, here],
            packed.at[group, steps, :, :, here],
            load_sem.at[group, part],
        )

    def mix(group):
        for part in range(3):
            finish(3, group, part)
            load(group, part).start()
        finish_own(3, group)
        for part in range(3):
            load(group, part).wait()
            here = back_cols(part)
            rows = packed[group, :, :, :, here].reshape(ROWS, BACK_PARTS[part][1])
            total = jnp.dot(mixes[group, part], rows, preferred_element_type=F32)
            if group:
                total = total + mixed[:, here]
            mixed[:, here] = total

    def mix_last(part, rest):
        here = stretch_cols(BACK_PARTS, part, rest)
        rows = last[:, :, :, here].reshape(ROWS, here.size)
        total = jnp.dot(mixes[GROUPS - 1, part], rows, preferred_element_type=F32) + mixed[:, here]
        mixed[:, here] = total
        lines[:, here] = total.astype(BF16)

    def relay5(part, step, rest):
        here = half_cols(BACK_PARTS, part, rest, RELAYED[step])
        return pltpu.make_async_remote_copy(
            src_ref=lines.at[pl.ds(2 * TOK, TOK), here],
            dst_ref=passing.at[:, here],
            send_sem=end_sem.at[0],
            recv_sem=pass_recv.at[rest, part, step // 2],
            device_id=peer(ORDERS[part][0], step),
            device_id_type=MESH,
        )

    def phase5(part, step, rest, half):
        here = half_cols(BACK_PARTS, part, rest, half)
        return pltpu.make_async_remote_copy(
            src_ref=lines.at[pl.ds(step * TOK, TOK), here],
            dst_ref=sums.at[(step + 1) // 2, :, here],
            send_sem=end_sem.at[0],
            recv_sem=end_sem.at[1],
            device_id=peer(ORDERS[part][0], step),
            device_id_type=MESH,
        )

    mix(0)
    finish_own(2, GROUPS - 1)
    for rest in range(2):
        for part in range(3):
            if rest == 0:
                finish(2, GROUPS - 1, part)
            start(3, GROUPS - 1, part, rest)
    start_own(3, GROUPS - 1)
    mix(1)
    finish_own(3, GROUPS - 1)
    for rest in range(2):
        for part in range(3):
            finish(3, GROUPS - 1, part, rest)
            mix_last(part, rest)
            for step in (1, 3):
                relay5(part, step, rest).start()
        for part in range(3):
            for step in (1, 3):
                phase5(part, step, rest, 1 - RELAYED[step]).start()
        for part in range(3):
            for step in (1, 3):
                here = half_cols(BACK_PARTS, part, rest, RELAYED[step])
                these = slice(step * TOK, (step + 1) * TOK)
                relay5(part, step, rest).wait_recv()
                lines[these, here] = (mixed[these, here] + passing[:, here].astype(F32)).astype(BF16)
                phase5(part, step, rest, RELAYED[step]).start()
    own5 = pltpu.make_async_copy(lines.at[pl.ds(0, TOK)], sums.at[0], x_sem.at[0])
    own5.start()
    wait_bytes(mid_ref.at[:, pl.ds(1, SIDE - 1)], hop_send.at[1, 0])
    wait_bytes(landed.at[:, pl.ds(1, SIDE - 1)], hop_send.at[2, 0])
    wait_bytes(back_ref.at[:, pl.ds(1, SIDE - 1)], hop_send.at[3, 0])
    own5.wait()
    wait_bytes(lines.at[pl.ds(0, 3 * TOK)], end_sem.at[0])
    wait_bytes(sums.at[pl.ds(1, 2)], end_sem.at[1])


def on_device(tokens, routes, gate_fixed, w_gate, w_up, w_down):
    big = jax.ShapeDtypeStruct((GROUPS, SIDE, SIDE, BLOCK, WIDTH), BF16)
    hbm = pl.BlockSpec(memory_space=pltpu.HBM)
    dma = pltpu.SemaphoreType.DMA
    sums, _, _, _ = pl.pallas_call(
        kernel,
        out_shape=(jax.ShapeDtypeStruct((3, TOK, WIDTH), BF16), big, big, big),
        in_specs=[hbm] * 6,
        out_specs=(hbm, hbm, hbm, hbm),
        scratch_shapes=[
            pltpu.VMEM((TOP, TOK), jnp.int32),
            pltpu.VMEM((TOP, TOK), jnp.int32),
            pltpu.VMEM((SIDE * TOK, WIDTH), BF16),
            pltpu.VMEM((TOK, WIDTH), BF16),
            pltpu.VMEM((SIDE, SIDE, BLOCK, WIDTH), BF16),
            pltpu.VMEM((3, SIDE * TOK, 2 * EXPERTS), BF16),
            pltpu.VMEM((GROUPS, SIDE, SIDE, BLOCK, WIDTH), BF16),
            pltpu.VMEM((GROUPS, SIDE, SIDE, BLOCK, WIDTH), BF16),
            pltpu.VMEM((ROWS, 2 * HALF), BF16),
            pltpu.VMEM((ROWS, 2 * HALF), BF16),
            pltpu.VMEM((GROUPS, 3, SIDE * TOK, ROWS), BF16),
            pltpu.VMEM((SIDE * TOK, WIDTH), F32),
            pltpu.VMEM((2, WIDTH, HALF), BF16),
            pltpu.VMEM((2, WIDTH, HALF), BF16),
            pltpu.VMEM((2, HALF, WIDTH), BF16),
            dma((4, GROUPS)),
            dma((4, GROUPS + 1, 3)),
            dma((1,)),
            dma((2, 3, 2)),
            dma((2, 3)),
            dma((2, 3, 2)),
            dma((2,)),
            dma((3,)),
            dma((3,)),
            dma((3,)),
            dma((3,)),
            dma((4, GROUPS)),
            dma((2, 3)),
            dma((3,)),
        ],
        compiler_params=pltpu.CompilerParams(
            collective_id=0, has_side_effects=True, vmem_limit_bytes=67043328
        ),
        name="moe",
    )(tokens, routes.T, gate_fixed.T, w_gate, w_up, w_down)
    return jnp.sum(sums.astype(F32), axis=0).astype(BF16)


def solution(mesh):
    split = P(("dp", "expert"), None)
    placed = (split, split, split) + (P(("dp", "expert"), None, None),) * 3
    return jax.shard_map(on_device, mesh=mesh, in_specs=placed, out_specs=split, check_vma=False)
```

```python
import jax
import jax.numpy as jnp
from jax import lax
from jax.experimental import pallas as pl
from jax.experimental.pallas import tpu as pltpu
from jax.sharding import PartitionSpec as P

MESH = pl.DeviceIdType.MESH
F32 = jnp.float32
BF16 = jnp.bfloat16

SIDE = 4
TOK = 64
TOP = 8
EXPERTS = 64
WIDTH = 4096
HALF = 768
GROUPS = 3
SLOTS = 4
BLOCK = SIDE * SLOTS
ROWS = SIDE * SIDE * BLOCK

PARTS = ((0, 1408), (1408, 1408), (2816, 1280))
BACK_PARTS = ((0, 1280), (1280, 1408), (2688, 1408))
ORDERS = ("yxz", "xzy", "zyx")
STEPS = (1, 3, 2)
CHUNK = 256


def nt(left, right):
    return lax.dot_general(left, right, (((1,), (1,)), ((), ())), preferred_element_type=F32)


def iota(shape, dim):
    return lax.broadcasted_iota(jnp.int32, shape, dim)


def ones_where(condition):
    return jnp.where(condition, 1.0, 0.0).astype(BF16)


def cols(part):
    return pl.ds(PARTS[part][0], PARTS[part][1])


def back_cols(part):
    return pl.ds(BACK_PARTS[part][0], BACK_PARTS[part][1])


RELAYED = {1: 0, 3: 1}


def stretch(parts, part, rest):
    first, size = parts[part]
    cut = 768 if parts is PARTS else size - 384
    return (first + cut, size - cut) if rest else (first, cut)


def stretch_cols(parts, part, rest):
    return pl.ds(*stretch(parts, part, rest))


def half_cols(parts, part, rest, half):
    first, size = stretch(parts, part, rest)
    cut = (size // 2 + 127) // 128 * 128
    return pl.ds(first + cut, size - cut) if half else pl.ds(first, cut)


def turn_matrix(forward):
    row = iota((ROWS, ROWS), 0)
    if forward:
        source = ((row >> 2) & 3) * 64 + (row >> 6) * 16 + ((row >> 4) & 3) * 4 + (row & 3)
    else:
        source = ((row >> 4) & 3) * 64 + ((row >> 2) & 3) * 16 + (row >> 6) * 4 + (row & 3)
    return ones_where(source == iota((ROWS, ROWS), 1))


def kernel(
    x_ref,
    routes_hbm,
    gate_hbm,
    wg_hbm,
    wu_hbm,
    wd_hbm,
    sums,
    mid_ref,
    back_ref,
    home_ref,
    routes_ref,
    gate_ref,
    lines,
    passing,
    last,
    tables,
    packed,
    landed,
    hidden,
    turned,
    mixes,
    mixed,
    wg,
    wu,
    wd,
    hop_send,
    hop_recv,
    start_send,
    first_recv,
    start_recv,
    pass_recv,
    end_sem,
    tab_sem,
    w_send,
    w_recv,
    w_local,
    own_sem,
    load_sem,
    x_sem,
):
    row = lax.axis_index("expert")
    at = {"y": lax.axis_index("dp"), "x": row // 8, "z": (row // 2) % 4}
    core = row % 2

    def device(where, which):
        return (where["y"], (where["x"] * 4 + where["z"]) * 2 + which)

    def peer(axis, shift):
        where = dict(at)
        where[axis] = (at[axis] + shift) % SIDE
        return device(where, core)

    partner = device(at, 1 - core)

    barrier = pltpu.get_barrier_semaphore()
    for step in (1, 3):
        for axis in "yxz":
            pl.semaphore_signal(barrier, inc=1, device_id=peer(axis, step), device_id_type=MESH)
    pl.semaphore_signal(barrier, inc=1, device_id=partner, device_id_type=MESH)

    def wait_bytes(ref, sem):
        pltpu.make_async_copy(ref, ref, sem).wait()

    own_rows = pltpu.make_async_copy(x_ref, lines.at[pl.ds(0, TOK)], x_sem.at[0])
    own_choices = [
        pltpu.make_async_copy(routes_hbm, routes_ref, x_sem.at[1]),
        pltpu.make_async_copy(gate_hbm, gate_ref, x_sem.at[2]),
    ]
    for copy in own_choices + [own_rows]:
        copy.start()
    own_weights = [
        pltpu.make_async_copy(src.at[0], dst.at[0], w_local.at[index])
        for index, (src, dst) in enumerate(((wg_hbm, wg), (wu_hbm, wu), (wd_hbm, wd)))
    ]

    pl.semaphore_wait(barrier, 7)

    def phase0(part, step, rest, half):
        here = half_cols(PARTS, part, rest, half)
        return pltpu.make_async_remote_copy(
            src_ref=x_ref.at[:, here],
            dst_ref=lines.at[pl.ds(step * TOK, TOK), here],
            send_sem=start_send.at[0],
            recv_sem=first_recv.at[rest, part, step // 2] if half == RELAYED[step] else start_recv.at[rest, part],
            device_id=peer(ORDERS[part][0], -step),
            device_id_type=MESH,
        )

    def relay0(part, step, rest):
        here = half_cols(PARTS, part, rest, RELAYED[step])
        return pltpu.make_async_remote_copy(
            src_ref=lines.at[pl.ds(step * TOK, TOK), here],
            dst_ref=lines.at[pl.ds(2 * TOK, TOK), here],
            send_sem=start_send.at[0],
            recv_sem=start_recv.at[rest, part],
            device_id=peer(ORDERS[part][0], -step),
            device_id_type=MESH,
        )

    def table_copy(part, step):
        origin = 1 if step == 2 else 0
        return pltpu.make_async_remote_copy(
            src_ref=tables.at[part, pl.ds(origin * TOK, TOK)],
            dst_ref=tables.at[part, pl.ds(step * TOK, TOK)],
            send_sem=tab_sem.at[0],
            recv_sem=tab_sem.at[1 if step == 1 else 2],
            device_id=peer(ORDERS[part][0], origin - step),
            device_id_type=MESH,
        )

    def start_tokens(rest, relayed):
        for step in (1, 3):
            for part in range(3):
                phase0(part, step, rest, RELAYED[step] if relayed else 1 - RELAYED[step]).start()

    def pass_on(rest):
        for part in range(3):
            for step in (1, 3):
                phase0(part, step, rest, RELAYED[step]).wait_recv()
                relay0(part, step, rest).start()

    start_tokens(0, True)
    start_tokens(0, False)
    for copy in own_choices:
        copy.wait()

    quant = gate_ref[...].astype(F32)
    weight = quant / jnp.sum(quant, axis=0, keepdims=True)
    named = jnp.zeros((EXPERTS, TOK), F32)
    share = jnp.zeros((EXPERTS, TOK), F32)
    for k in range(TOP):
        hit = routes_ref[k : k + 1, :] == iota((EXPERTS, TOK), 0)
        named = named + jnp.where(hit, 1.0, 0.0)
        share = share + jnp.where(hit, weight[k : k + 1, :], 0.0)
    earlier = ones_where(iota((TOK, TOK), 0) < iota((TOK, TOK), 1))
    before = jnp.dot(named.astype(BF16), earlier, preferred_element_type=F32)
    slots = jnp.where(named > 0.5, before, -1.0)
    own_table = jnp.concatenate([slots, share], axis=0).T.astype(BF16)
    for part in range(3):
        tables[part, 0:TOK, :] = own_table

    for step in (1, 3):
        for part in range(3):
            table_copy(part, step).start()
    start_tokens(1, True)

    other_weights = [
        pltpu.make_async_remote_copy(
            src_ref=src.at[0],
            dst_ref=dst.at[1],
            send_sem=w_send.at[index],
            recv_sem=w_recv.at[index],
            device_id=partner,
            device_id_type=MESH,
        )
        for index, (src, dst) in enumerate(((wg_hbm, wg), (wu_hbm, wu), (wd_hbm, wd)))
    ]

    def chosen(part):
        index = iota((ROWS, EXPERTS), 0)
        a, b, c = (at[axis] for axis in ORDERS[part])
        where = dict(zip(ORDERS[part], (a, (b - (index >> 6)) & 3, (c - ((index >> 4) & 3)) & 3)))
        expert = where["y"] * 16 + where["x"] * 4 + where["z"]
        return ones_where(expert == iota((ROWS, EXPERTS), 1))

    def ends(phase, group, step, here):
        if phase == 0:
            return packed.at[group, step, :, :, here], mid_ref.at[group, :, step, :, here]
        if phase == 1:
            return mid_ref.at[group, step, :, :, here], landed.at[group, step, :, :, here]
        if phase == 2:
            return landed.at[group, step, :, :, here], back_ref.at[group, :, step, :, here]
        if group == GROUPS - 1:
            return back_ref.at[group, step, :, :, here], last.at[step, :, :, here]
        return back_ref.at[group, step, :, :, here], home_ref.at[group, step, :, :, here]

    def part_cols(phase, part, rest):
        parts = PARTS if phase < 2 else BACK_PARTS
        return pl.ds(*(parts[part] if rest is None else stretch(parts, part, rest)))

    def start(phase, group, part, rest=None):
        axis = ORDERS[part][1 if phase in (0, 3) else 2]
        for step in STEPS:
            src, dst = ends(phase, group, step, part_cols(phase, part, rest))
            pltpu.make_async_remote_copy(
                src_ref=src,
                dst_ref=dst,
                send_sem=hop_send.at[phase, group if phase == 0 else 0],
                recv_sem=hop_recv.at[phase, GROUPS if rest else group, part],
                device_id=peer(axis, step if phase > 1 else -step),
                device_id_type=MESH,
            ).start()

    def finish(phase, group, part, rest=None):
        _, dst = ends(phase, group, pl.ds(1, SIDE - 1), part_cols(phase, part, rest))
        wait_bytes(dst, hop_recv.at[phase, GROUPS if rest else group, part])

    def own_hop(phase, group):
        src, dst = ends(phase, group, 0, pl.ds(0, WIDTH))
        if phase == 3 and group < GROUPS - 1:
            dst = packed.at[group, 0]
        return pltpu.make_async_copy(src, dst, own_sem.at[phase, group])

    def start_own(phase, group):
        own_hop(phase, group).start()

    def finish_own(phase, group):
        own_hop(phase, group).wait()

    def finish_all(phase, group):
        finish_own(phase, group)
        for part in range(3):
            finish(phase, group, part)

    def gather(group, part, rest=None):
        first, size = PARTS[part] if rest is None else stretch(PARTS, part, rest)
        found = nt(chosen(part), tables[part, :, 0:EXPERTS])
        row = iota((ROWS, SIDE * TOK), 0)
        slot = (row & 3) + group * SLOTS
        holder = iota((ROWS, SIDE * TOK), 1) >> 6
        pick = ones_where((found == slot.astype(F32)) & (holder == ((row >> 2) & 3)))
        rows = jnp.dot(pick, lines[:, first : first + size], preferred_element_type=F32)
        packed[group, :, :, :, first : first + size] = rows.astype(BF16).reshape(SIDE, SIDE, BLOCK, size)

    def mix_tables(part):
        select = chosen(part)
        found = nt(tables[part, :, 0:EXPERTS], select)
        scale = nt(tables[part, :, EXPERTS : 2 * EXPERTS], select)
        col = iota((SIDE * TOK, ROWS), 1)
        mine = (iota((SIDE * TOK, ROWS), 0) >> 6) == ((col >> 2) & 3)
        for group in range(GROUPS):
            slot = (col & 3) + group * SLOTS
            mixes[group, part] = jnp.where((found == slot.astype(F32)) & mine, scale, 0.0).astype(BF16)

    wait_bytes(tables.at[:, pl.ds(0, TOK)], tab_sem.at[1])
    for part in range(3):
        table_copy(part, 2).start()
    pass_on(0)
    start_tokens(1, False)
    for copy in own_weights + other_weights:
        copy.start()
    own_rows.wait()
    pass_on(1)
    wait_bytes(tables.at[:, pl.ds(0, 2 * TOK)], tab_sem.at[2])
    for rest in range(2):
        for part in range(3):
            here = stretch_cols(PARTS, part, rest)
            wait_bytes(lines.at[pl.ds(0, 2 * TOK), here], start_recv.at[rest, part])
            gather(0, part, rest)
            start(0, 0, part, rest)
    start_own(0, 0)
    for part in range(3):
        gather(1, part)
        start(0, 1, part)
    start_own(0, 1)
    for part in range(3):
        gather(2, part)
    finish_own(0, 0)
    for part in range(3):
        finish(0, 0, part, 0)
        finish(0, 0, part, 1)
        start(1, 0, part)
    start_own(1, 0)
    for part in range(3):
        start(0, 2, part)
    start_own(0, 2)
    for part in range(3):
        mix_tables(part)
    wait_bytes(tables.at[:, pl.ds(0, 3 * TOK)], tab_sem.at[0])
    wait_bytes(lines.at[pl.ds(0, 3 * TOK)], start_send.at[0])
    finish_own(0, 1)
    for part in range(3):
        finish(0, 1, part)
        start(1, 1, part)
    start_own(1, 1)

    def arrange(group):
        for part in range(3):
            first, size = PARTS[part]
            rows = landed[group, :, :, :, first : first + size]
            if part:
                rows = rows.reshape(ROWS, size)
                rows = jnp.dot(turn_matrix(part == 1), rows, preferred_element_type=F32)
                rows = rows.astype(BF16).reshape(SIDE, SIDE, BLOCK, size)
            packed[group, :, :, :, first : first + size] = rows

    def inner(group):
        @pl.loop(0, 2 * HALF // CHUNK)
        def _(index):
            side = index // (HALF // CHUNK)
            these = pl.ds(pl.multiple_of((index % (HALF // CHUNK)) * CHUNK, CHUNK), CHUNK)
            those = pl.ds(pl.multiple_of(index * CHUNK, CHUNK), CHUNK)
            rows = packed[group].reshape(ROWS, WIDTH)
            gate = jnp.dot(rows, wg[side, :, these], preferred_element_type=F32)
            upper = jnp.dot(rows, wu[side, :, these], preferred_element_type=F32)
            hidden[:, those] = (gate / (1.0 + jnp.exp(-gate)) * upper).astype(BF16)

    def outer(group, part):
        first, size = BACK_PARTS[part]
        source = hidden
        if part:
            turned[...] = jnp.dot(
                turn_matrix(part == 2), hidden[...], preferred_element_type=F32
            ).astype(BF16)
            source = turned
        for begin in range(first, first + size, CHUNK):
            end = min(begin + CHUNK, first + size)
            total = jnp.dot(source[:, :HALF], wd[0, :, begin:end], preferred_element_type=F32)
            total = total + jnp.dot(source[:, HALF:], wd[1, :, begin:end], preferred_element_type=F32)
            landed[group, :, :, :, begin:end] = total.astype(BF16).reshape(SIDE, SIDE, BLOCK, end - begin)

    for copy in own_weights + other_weights:
        copy.wait()

    for group in range(GROUPS):
        finish_all(1, group)
        wait_bytes(packed.at[group, pl.ds(1, SIDE - 1)], hop_send.at[0, group])
        arrange(group)
        inner(group)
        if group == 0:
            finish_own(0, 2)
            for part in range(3):
                finish(0, 2, part)
                start(1, 2, part)
            start_own(1, 2)
        for part in range(3):
            outer(group, part)
            start(2, group, part)
        start_own(2, group)
        if group:
            finish_own(2, group - 1)
            for part in range(3):
                finish(2, group - 1, part)
                start(3, group - 1, part)
            start_own(3, group - 1)

    def load(group, part):
        here = back_cols(part)
        steps = pl.ds(1, SIDE - 1)
        return pltpu.make_async_copy(
            home_ref.at[group, steps, :, :, here],
            packed.at[group, steps, :, :, here],
            load_sem.at[group, part],
        )

    def mix(group):
        for part in range(3):
            finish(3, group, part)
            load(group, part).start()
        finish_own(3, group)
        for part in range(3):
            load(group, part).wait()
            here = back_cols(part)
            rows = packed[group, :, :, :, here].reshape(ROWS, BACK_PARTS[part][1])
            total = jnp.dot(mixes[group, part], rows, preferred_element_type=F32)
            if group:
                total = total + mixed[:, here]
            mixed[:, here] = total

    def mix_last(part, rest):
        here = stretch_cols(BACK_PARTS, part, rest)
        rows = last[:, :, :, here].reshape(ROWS, here.size)
        total = jnp.dot(mixes[GROUPS - 1, part], rows, preferred_element_type=F32) + mixed[:, here]
        mixed[:, here] = total
        lines[:, here] = total.astype(BF16)

    def relay5(part, step, rest):
        here = half_cols(BACK_PARTS, part, rest, RELAYED[step])
        return pltpu.make_async_remote_copy(
            src_ref=lines.at[pl.ds(2 * TOK, TOK), here],
            dst_ref=passing.at[:, here],
            send_sem=end_sem.at[0],
            recv_sem=pass_recv.at[rest, part, step // 2],
            device_id=peer(ORDERS[part][0], step),
            device_id_type=MESH,
        )

    def phase5(part, step, rest, half):
        here = half_cols(BACK_PARTS, part, rest, half)
        return pltpu.make_async_remote_copy(
            src_ref=lines.at[pl.ds(step * TOK, TOK), here],
            dst_ref=sums.at[(step + 1) // 2, :, here],
            send_sem=end_sem.at[0],
            recv_sem=end_sem.at[1],
            device_id=peer(ORDERS[part][0], step),
            device_id_type=MESH,
        )

    mix(0)
    finish_own(2, GROUPS - 1)
    for rest in range(2):
        for part in range(3):
            if rest == 0:
                finish(2, GROUPS - 1, part)
            start(3, GROUPS - 1, part, rest)
    start_own(3, GROUPS - 1)
    mix(1)
    finish_own(3, GROUPS - 1)
    for rest in range(2):
        for part in range(3):
            finish(3, GROUPS - 1, part, rest)
            mix_last(part, rest)
            for step in (1, 3):
                relay5(part, step, rest).start()
        if rest == 0:
            for part in range(3):
                for step in (1, 3):
                    phase5(part, step, rest, 1 - RELAYED[step]).start()
    for rest in range(2):
        for part in range(3):
            for step in (1, 3):
                here = half_cols(BACK_PARTS, part, rest, RELAYED[step])
                these = slice(step * TOK, (step + 1) * TOK)
                relay5(part, step, rest).wait_recv()
                lines[these, here] = (mixed[these, here] + passing[:, here].astype(F32)).astype(BF16)
                phase5(part, step, rest, RELAYED[step]).start()
        if rest == 0:
            for part in range(3):
                for step in (1, 3):
                    phase5(part, step, 1, 1 - RELAYED[step]).start()
    own5 = pltpu.make_async_copy(lines.at[pl.ds(0, TOK)], sums.at[0], x_sem.at[0])
    own5.start()
    wait_bytes(mid_ref.at[:, pl.ds(1, SIDE - 1)], hop_send.at[1, 0])
    wait_bytes(landed.at[:, pl.ds(1, SIDE - 1)], hop_send.at[2, 0])
    wait_bytes(back_ref.at[:, pl.ds(1, SIDE - 1)], hop_send.at[3, 0])
    own5.wait()
    wait_bytes(lines.at[pl.ds(0, 3 * TOK)], end_sem.at[0])
    wait_bytes(sums.at[pl.ds(1, 2)], end_sem.at[1])


def on_device(tokens, routes, gate_fixed, w_gate, w_up, w_down):
    big = jax.ShapeDtypeStruct((GROUPS, SIDE, SIDE, BLOCK, WIDTH), BF16)
    hbm = pl.BlockSpec(memory_space=pltpu.HBM)
    dma = pltpu.SemaphoreType.DMA
    sums, _, _, _ = pl.pallas_call(
        kernel,
        out_shape=(jax.ShapeDtypeStruct((3, TOK, WIDTH), BF16), big, big, big),
        in_specs=[hbm] * 6,
        out_specs=(hbm, hbm, hbm, hbm),
        scratch_shapes=[
            pltpu.VMEM((TOP, TOK), jnp.int32),
            pltpu.VMEM((TOP, TOK), jnp.int32),
            pltpu.VMEM((SIDE * TOK, WIDTH), BF16),
            pltpu.VMEM((TOK, WIDTH), BF16),
            pltpu.VMEM((SIDE, SIDE, BLOCK, WIDTH), BF16),
            pltpu.VMEM((3, SIDE * TOK, 2 * EXPERTS), BF16),
            pltpu.VMEM((GROUPS, SIDE, SIDE, BLOCK, WIDTH), BF16),
            pltpu.VMEM((GROUPS, SIDE, SIDE, BLOCK, WIDTH), BF16),
            pltpu.VMEM((ROWS, 2 * HALF), BF16),
            pltpu.VMEM((ROWS, 2 * HALF), BF16),
            pltpu.VMEM((GROUPS, 3, SIDE * TOK, ROWS), BF16),
            pltpu.VMEM((SIDE * TOK, WIDTH), F32),
            pltpu.VMEM((2, WIDTH, HALF), BF16),
            pltpu.VMEM((2, WIDTH, HALF), BF16),
            pltpu.VMEM((2, HALF, WIDTH), BF16),
            dma((4, GROUPS)),
            dma((4, GROUPS + 1, 3)),
            dma((1,)),
            dma((2, 3, 2)),
            dma((2, 3)),
            dma((2, 3, 2)),
            dma((2,)),
            dma((3,)),
            dma((3,)),
            dma((3,)),
            dma((3,)),
            dma((4, GROUPS)),
            dma((2, 3)),
            dma((3,)),
        ],
        compiler_params=pltpu.CompilerParams(
            collective_id=0, has_side_effects=True, vmem_limit_bytes=67043328
        ),
        name="moe",
    )(tokens, routes.T, gate_fixed.T, w_gate, w_up, w_down)
    return jnp.sum(sums.astype(F32), axis=0).astype(BF16)


def solution(mesh):
    split = P(("dp", "expert"), None)
    placed = (split, split, split) + (P(("dp", "expert"), None, None),) * 3
    return jax.shard_map(on_device, mesh=mesh, in_specs=placed, out_specs=split, check_vma=False)
```
